256 devices in a mesh: expert: 64 (over z, x, core), tensor: 4 (over y).
Axes of the slice: x: 4, y: 4, z: 8, core: 2. Of those that a mesh axis runs over, the one named last changes fastest.
Arguments:
- tokens: bfloat16 [2048, 4096], P('expert', 'tensor'), may hold values from -6 to 6
- cotangent: bfloat16 [2048, 4096], P('expert', 'tensor'), may hold values from -6 to 6
- routing: int32 [2048, 8], P('expert'), may hold values from 0 to 63, as said below
- gates: float32 [2048, 8], P('expert'), may hold values from 0.1 to 0.4
- w_in: bfloat16 [64, 4096, 1536], P('expert', None, 'tensor'), may hold values from -0.09375 to 0.09375
- w_out: bfloat16 [64, 1536, 4096], P('expert', 'tensor'), may hold values from -0.15625 to 0.15625
Outputs:
- mixed: bfloat16 [2048, 4096], P('expert', 'tensor')
- d_tokens: bfloat16 [2048, 4096], P('expert', 'tensor')
- d_w_in: bfloat16 [64, 4096, 1536], P('expert', None, 'tensor')
- d_w_out: bfloat16 [64, 1536, 4096], P('expert', 'tensor')
The draws below stay inside these ranges and needn't reach their ends.
Inputs may be any that keep to these rules, and one draw needn't show every extreme that they name: `routing`: each row names 8 different experts. In each aligned block of 32 rows (the tokens of one index of the expert axis) no expert is named by more than 8 rows, and one expert is named by exactly 8 rows of every block.
All inputs are finite; a program needn't handle non-finite values.
Results may differ from the reference program's by a relative error of at most 0.0058.
Values may be sent and summed in bfloat16 or wider, within the bound.
A program may use at most 128 MiB of HBM per device.

```python
import jax
import jax.numpy as jnp
from jax import lax

D = 4096
FF = 1536
EXPERTS = 64
TOP = 8
TOK_DEV = 32
SLOT = 8
TOKENS = 2048


def draw_routing(key, part):
    block_count = TOKENS // TOK_DEV
    busy_key, rest_key = jax.random.split(key)
    busiest = jax.random.randint(busy_key, (), 0, EXPERTS, dtype=jnp.int32)
    columns = jnp.arange(TOP, dtype=jnp.int32)

    def one_block(block_key):
        subkeys = jax.random.split(block_key, 4)
        shuffled = jax.random.permutation(subkeys[0], TOK_DEV).astype(jnp.int32)
        inverse = jnp.zeros((TOK_DEV,), jnp.int32).at[shuffled].set(jnp.arange(TOK_DEV, dtype=jnp.int32))
        is_busy = (inverse < SLOT).astype(jnp.int32)
        others = jax.random.permutation(subkeys[1], EXPERTS - 1).astype(jnp.int32)
        others = others + (others >= busiest).astype(jnp.int32)
        period = jax.random.randint(subkeys[2], (), 4 * TOP, EXPERTS, dtype=jnp.int32)
        demand = TOP - is_busy
        offset = (jnp.cumsum(demand) - demand).astype(jnp.int32)
        position = offset[:, None] + columns[None, :] - is_busy[:, None]
        chosen = others[jnp.mod(position, period)]
        chosen = jnp.where((is_busy[:, None] == 1) & (columns[None, :] == 0), busiest, chosen)
        rotation = jax.random.randint(subkeys[3], (TOK_DEV,), 0, TOP, dtype=jnp.int32)
        rolled = jnp.mod(columns[None, :] + rotation[:, None], TOP)
        return jnp.take_along_axis(chosen, rolled, axis=1)
    blocks = jax.vmap(one_block)(jax.random.split(rest_key, block_count))
    return blocks.reshape(TOKENS, TOP).astype(jnp.int32)


def level_of(own_key, shape, cuts, low, high):
    factor_of = 1.0
    for dim, shards_of in cuts:
        steps = jax.random.uniform(jax.random.fold_in(jax.random.fold_in(own_key, 6), dim), (shards_of,), jnp.float32, low / len(cuts), high / len(cuts))
        factor_of = factor_of * jnp.repeat(jnp.exp(steps), shape[dim] // shards_of).reshape((-1,) + (1,) * (len(shape) - 1 - dim))
    return factor_of


def gaussian(own_key, extent, width, reach, cuts=(), kind=jnp.bfloat16):
    drawn = jax.random.normal(own_key, extent, jnp.float32) * width
    if len(cuts) > 0:
        drawn = level_of(own_key, extent, cuts, -0.22, 0.18) * drawn
    return jnp.clip(drawn, min=-reach, max=reach).astype(kind)


def setup_inputs(seed: int = 0) -> dict:
    key_of = jax.random.split(jax.random.key(seed), 7)
    return {
        "tokens": gaussian(key_of[0], (TOKENS, D), 1.0, 6.0, ((0, 64), (1, 4))),
        "cotangent": gaussian(key_of[1], (TOKENS, D), 1.0, 6.0, ((0, 64), (1, 4))),
        "routing": draw_routing(jax.random.fold_in(key_of[6], 71), 0),
        "gates": jnp.clip(0.1 + 0.3 * jax.random.uniform(key_of[3], (TOKENS, TOP), jnp.float32) ** level_of(key_of[3], (TOKENS, TOP), ((0, 64),), -0.2, 0.2), 0.1, 0.4),
        "w_in": gaussian(key_of[4], (EXPERTS, D, FF), D ** -0.5, 0.09375, ((0, 64), (2, 4))),
        "w_out": gaussian(key_of[5], (EXPERTS, FF, D), FF ** -0.5, 0.15625, ((0, 64), (1, 4))),
    }


row_tile = 64


def reference(tokens, cotangent, routing, gates, w_in, w_out):
    pair_total = TOKENS * TOP
    flat_routes = routing.reshape(-1).astype(jnp.int32)
    sorted_pairs = jnp.argsort(flat_routes, stable=True).astype(jnp.int32)
    expert_load = jnp.sum((flat_routes[None, :] == jnp.arange(EXPERTS, dtype=jnp.int32)[:, None]).astype(jnp.int32), axis=1).astype(jnp.int32)
    row_first = (jnp.cumsum(expert_load) - expert_load).astype(jnp.int32)
    padded_pairs = jnp.concatenate([sorted_pairs, jnp.zeros((row_tile,), jnp.int32)])
    gate_flat = gates.reshape(-1)

    def expert_step(carry, inputs):
        out_pairs, grad_pairs = carry
        weight_in, weight_out, first_row, row_count = inputs

        def tile_step(tile, state):
            out_acc, grad_acc, grad_in, grad_out = state
            offset = (first_row + tile * row_tile).astype(jnp.int32)
            pair_ids = lax.dynamic_slice(padded_pairs, (offset,), (row_tile,))
            usable = (jnp.arange(row_tile, dtype=jnp.int32) + tile * row_tile) < row_count
            token_rows = pair_ids // TOP
            inputs_tile = jnp.where(usable[:, None], tokens[token_rows], jnp.zeros((), tokens.dtype)).astype(tokens.dtype)
            gate_rows = jnp.where(usable, gate_flat[pair_ids], jnp.zeros((), jnp.float32))
            scaled_cot = (gate_rows[:, None] * cotangent[token_rows].astype(jnp.float32)).astype(jnp.bfloat16)
            preact = jnp.dot(inputs_tile, weight_in, preferred_element_type=jnp.float32)
            sigmoid_val = jax.nn.sigmoid(preact)
            hidden = (preact * sigmoid_val).astype(jnp.bfloat16)
            outputs = jnp.dot(hidden, weight_out, preferred_element_type=jnp.float32)
            grad_hidden = jnp.dot(scaled_cot, weight_out.T, preferred_element_type=jnp.float32)
            grad_preact = (grad_hidden * sigmoid_val * (1.0 + preact * (1.0 - sigmoid_val))).astype(jnp.bfloat16)
            grad_rows = jnp.dot(grad_preact, weight_in.T, preferred_element_type=jnp.float32)
            grad_out = grad_out + jnp.dot(hidden.T, scaled_cot, preferred_element_type=jnp.float32)
            grad_in = grad_in + jnp.dot(inputs_tile.T, grad_preact, preferred_element_type=jnp.float32)
            out_acc = out_acc.at[pair_ids].add(jnp.where(usable[:, None], outputs, jnp.zeros((), jnp.float32)))
            grad_acc = grad_acc.at[pair_ids].add(jnp.where(usable[:, None], grad_rows, jnp.zeros((), jnp.float32)))
            return out_acc, grad_acc, grad_in, grad_out

        tile_count = ((row_count + row_tile - 1) // row_tile).astype(jnp.int32)
        start_state = (out_pairs, grad_pairs, jnp.zeros((D, FF), jnp.float32), jnp.zeros((FF, D), jnp.float32))
        result = lax.fori_loop(jnp.zeros((), jnp.int32), tile_count, tile_step, start_state)
        return (result[0], result[1]), (result[2].astype(jnp.bfloat16), result[3].astype(jnp.bfloat16))

    start_carry = (jnp.zeros((pair_total, D), jnp.float32), jnp.zeros((pair_total, D), jnp.float32))
    (out_pairs, grad_pairs), (d_w_in, d_w_out) = lax.scan(expert_step, start_carry, (w_in, w_out, row_first, expert_load))
    mixed = jnp.sum(gates[:, :, None] * out_pairs.reshape(TOKENS, TOP, D), axis=1).astype(jnp.bfloat16)
    d_tokens = jnp.sum(grad_pairs.reshape(TOKENS, TOP, D), axis=1).astype(jnp.bfloat16)
    return (mixed, d_tokens, d_w_in, d_w_out)
```

```python
import jax
import jax.numpy as jnp
from jax import lax
from jax.sharding import PartitionSpec as P


def shards(tokens, cotangent, routing, gates, w_in, w_out):
    devices = lax.axis_size("expert")
    local_experts = w_in.shape[0]
    experts = devices * local_experts
    tok_rows = routing.shape[0]
    capacity = tok_rows // 4
    buffer_rows = experts * capacity
    highest = lax.Precision.HIGHEST
    matches = (routing[:, :, None] == jnp.arange(experts, dtype=jnp.int32)[None, None, :]).astype(
        jnp.int32
    )
    per_token = jnp.sum(matches, axis=1)
    earlier = jnp.cumsum(per_token, axis=0) - per_token
    destination = routing * capacity + jnp.take_along_axis(earlier, routing, axis=1)
    placed = (
        destination[:, :, None] == jnp.arange(buffer_rows, dtype=jnp.int32)[None, None, :]
    ).astype(jnp.float32)
    membership = jnp.sum(placed, axis=1)
    weighting = jnp.sum(placed * gates[:, :, None], axis=1)
    quarter = tokens.shape[1]
    rows = jnp.einsum(
        "tr,td->rd",
        membership.astype(jnp.bfloat16),
        tokens,
        preferred_element_type=jnp.float32,
    ).astype(jnp.bfloat16)
    scaled = jnp.einsum(
        "tr,td->rd", weighting, cotangent.astype(jnp.float32), precision=highest
    ).astype(jnp.bfloat16)
    send = jnp.concatenate(
        [
            rows.reshape(devices, local_experts, capacity, quarter),
            scaled.reshape(devices, local_experts, capacity, quarter),
        ],
        axis=2,
    )
    arrived = lax.all_to_all(send, "expert", split_axis=0, concat_axis=0, tiled=True)
    whole = lax.all_gather(arrived, "tensor", axis=3, tiled=True)
    expert_rows = whole[:, :, :capacity]
    expert_scaled = whole[:, :, capacity:]
    preact = jnp.einsum("nesd,edh->nesh", expert_rows, w_in, preferred_element_type=jnp.float32)
    sigmoid_val = jax.nn.sigmoid(preact)
    hidden = (preact * sigmoid_val).astype(jnp.bfloat16)
    out_part = jnp.einsum("nesh,ehd->nesd", hidden, w_out, preferred_element_type=jnp.float32)
    grad_hidden = jnp.einsum(
        "nesd,ehd->nesh", expert_scaled, w_out, preferred_element_type=jnp.float32
    )
    grad_preact = (grad_hidden * sigmoid_val * (1.0 + preact * (1.0 - sigmoid_val))).astype(
        jnp.bfloat16
    )
    d_w_out = jnp.einsum(
        "nesh,nesd->ehd", hidden, expert_scaled, preferred_element_type=jnp.float32
    ).astype(jnp.bfloat16)
    d_w_in = jnp.einsum(
        "nesd,nesh->edh", expert_rows, grad_preact, preferred_element_type=jnp.float32
    ).astype(jnp.bfloat16)
    grad_part = jnp.einsum("nesh,edh->nesd", grad_preact, w_in, preferred_element_type=jnp.float32)
    parts = jnp.concatenate(
        [out_part.astype(jnp.bfloat16), grad_part.astype(jnp.bfloat16)], axis=2
    )
    sums = lax.psum_scatter(parts, "tensor", scatter_dimension=3, tiled=True)
    back = lax.all_to_all(sums, "expert", split_axis=0, concat_axis=0, tiled=True)
    back_out = back[:, :, :capacity].reshape(buffer_rows, quarter).astype(jnp.float32)
    back_grad = back[:, :, capacity:].reshape(buffer_rows, quarter).astype(jnp.float32)
    mixed = jnp.einsum("tr,rd->td", weighting, back_out, precision=highest).astype(jnp.bfloat16)
    d_tokens = jnp.einsum("tr,rd->td", membership, back_grad, precision=highest).astype(
        jnp.bfloat16
    )
    return (mixed, d_tokens, d_w_in, d_w_out)


def solution(mesh):
    placed = (
        P("expert", "tensor"),
        P("expert", "tensor"),
        P("expert", None),
        P("expert", None),
        P("expert", None, "tensor"),
        P("expert", "tensor", None),
    )
    return jax.shard_map(
        shards,
        mesh=mesh,
        in_specs=placed,
        out_specs=(
            P("expert", "tensor"),
            P("expert", "tensor"),
            P("expert", None, "tensor"),
            P("expert", "tensor", None),
        ),
        check_vma=False,
    )
```

```python
import jax
import jax.numpy as jnp
from jax import lax
from jax.sharding import PartitionSpec as P

CHUNKS = 2


def expert_chunk(rows, scaled, w_in, w_out, quarter):
    slots = rows.shape[2]
    send = jnp.concatenate([rows, scaled], axis=2)
    arrived = lax.all_to_all(send, "expert", split_axis=0, concat_axis=0, tiled=True)
    whole = lax.all_gather(arrived, "tensor", axis=3, tiled=True)
    expert_rows = whole[:, :, :slots]
    expert_scaled = whole[:, :, slots:]
    preact = jnp.einsum("nesd,edh->nesh", expert_rows, w_in, preferred_element_type=jnp.float32)
    sigmoid_val = jax.nn.sigmoid(preact)
    hidden = (preact * sigmoid_val).astype(jnp.bfloat16)
    out_part = jnp.einsum("nesh,ehd->nesd", hidden, w_out, preferred_element_type=jnp.float32)
    grad_hidden = jnp.einsum(
        "nesd,ehd->nesh", expert_scaled, w_out, preferred_element_type=jnp.float32
    )
    grad_preact = (grad_hidden * sigmoid_val * (1.0 + preact * (1.0 - sigmoid_val))).astype(
        jnp.bfloat16
    )
    d_w_out = jnp.einsum(
        "nesh,nesd->ehd", hidden, expert_scaled, preferred_element_type=jnp.float32
    )
    d_w_in = jnp.einsum(
        "nesd,nesh->edh", expert_rows, grad_preact, preferred_element_type=jnp.float32
    )
    grad_part = jnp.einsum("nesh,edh->nesd", grad_preact, w_in, preferred_element_type=jnp.float32)
    parts = jnp.concatenate(
        [out_part.astype(jnp.bfloat16), grad_part.astype(jnp.bfloat16)], axis=2
    )
    sums = lax.psum_scatter(parts, "tensor", scatter_dimension=3, tiled=True)
    back = lax.all_to_all(sums, "expert", split_axis=0, concat_axis=0, tiled=True)
    return back[:, :, :slots], back[:, :, slots:], d_w_in, d_w_out


def shards(tokens, cotangent, routing, gates, w_in, w_out):
    devices = lax.axis_size("expert")
    local_experts = w_in.shape[0]
    experts = devices * local_experts
    tok_rows = routing.shape[0]
    capacity = tok_rows // 4
    buffer_rows = experts * capacity
    highest = lax.Precision.HIGHEST
    matches = (routing[:, :, None] == jnp.arange(experts, dtype=jnp.int32)[None, None, :]).astype(
        jnp.int32
    )
    per_token = jnp.sum(matches, axis=1)
    earlier = jnp.cumsum(per_token, axis=0) - per_token
    destination = routing * capacity + jnp.take_along_axis(earlier, routing, axis=1)
    placed = (
        destination[:, :, None] == jnp.arange(buffer_rows, dtype=jnp.int32)[None, None, :]
    ).astype(jnp.float32)
    membership = jnp.sum(placed, axis=1)
    weighting = jnp.sum(placed * gates[:, :, None], axis=1)
    quarter = tokens.shape[1]
    rows = jnp.einsum(
        "tr,td->rd",
        membership.astype(jnp.bfloat16),
        tokens,
        preferred_element_type=jnp.float32,
    ).astype(jnp.bfloat16)
    scaled = jnp.einsum(
        "tr,td->rd", weighting, cotangent.astype(jnp.float32), precision=highest
    ).astype(jnp.bfloat16)
    rows = rows.reshape(devices, local_experts, capacity, quarter)
    scaled = scaled.reshape(devices, local_experts, capacity, quarter)
    step = capacity // CHUNKS
    back_out, back_grad, d_w_in, d_w_out = [], [], None, None
    for c in range(CHUNKS):
        window = slice(c * step, (c + 1) * step)
        with jax.named_scope(f"slot_chunk{c}"):
            b_out, b_grad, g_in, g_out = expert_chunk(
                rows[:, :, window], scaled[:, :, window], w_in, w_out, quarter
            )
        back_out.append(b_out)
        back_grad.append(b_grad)
        d_w_in = g_in if d_w_in is None else d_w_in + g_in
        d_w_out = g_out if d_w_out is None else d_w_out + g_out
    back_out = jnp.concatenate(back_out, axis=2).reshape(buffer_rows, quarter).astype(jnp.float32)
    back_grad = jnp.concatenate(back_grad, axis=2).reshape(buffer_rows, quarter).astype(jnp.float32)
    mixed = jnp.einsum("tr,rd->td", weighting, back_out, precision=highest).astype(jnp.bfloat16)
    d_tokens = jnp.einsum("tr,rd->td", membership, back_grad, precision=highest).astype(
        jnp.bfloat16
    )
    return (mixed, d_tokens, d_w_in.astype(jnp.bfloat16), d_w_out.astype(jnp.bfloat16))


def solution(mesh):
    placed = (
        P("expert", "tensor"),
        P("expert", "tensor"),
        P("expert", None),
        P("expert", None),
        P("expert", None, "tensor"),
        P("expert", "tensor", None),
    )
    return jax.shard_map(
        shards,
        mesh=mesh,
        in_specs=placed,
        out_specs=(
            P("expert", "tensor"),
            P("expert", "tensor"),
            P("expert", None, "tensor"),
            P("expert", "tensor", None),
        ),
        check_vma=False,
    )
```

```python
import jax
import jax.numpy as jnp
from jax import lax
from jax.experimental import pallas as pl
from jax.experimental.pallas import tpu as pltpu
from jax.sharding import PartitionSpec as P

CHUNKS = 2


def _a2a_kernel(x_ref, o_ref, send_sem, recv_sem, local_sem):
    n = x_ref.shape[0]
    me = lax.axis_index("expert")
    tau = lax.axis_index("tensor")
    barrier = pltpu.get_barrier_semaphore()

    def greet(k, carry):
        peer = lax.rem(me + k, n)
        pl.semaphore_signal(
            barrier, inc=1, device_id=(peer, tau), device_id_type=pl.DeviceIdType.MESH
        )
        return carry

    lax.fori_loop(1, n, greet, 0)
    pl.semaphore_wait(barrier, n - 1)

    local = pltpu.make_async_copy(x_ref.at[me], o_ref.at[me], local_sem)
    local.start()

    def push(k, carry):
        peer = lax.rem(me + k, n)
        pltpu.make_async_remote_copy(
            src_ref=x_ref.at[peer],
            dst_ref=o_ref.at[me],
            send_sem=send_sem.at[k],
            recv_sem=recv_sem.at[k],
            device_id=(peer, tau),
            device_id_type=pl.DeviceIdType.MESH,
        ).start()
        return carry

    lax.fori_loop(1, n, push, 0)

    def settle(k, carry):
        peer = lax.rem(me + k, n)
        source = lax.rem(me + n - k, n)
        pltpu.make_async_remote_copy(
            src_ref=x_ref.at[peer],
            dst_ref=o_ref.at[source],
            send_sem=send_sem.at[k],
            recv_sem=recv_sem.at[k],
            device_id=(peer, tau),
            device_id_type=pl.DeviceIdType.MESH,
        ).wait()
        return carry

    lax.fori_loop(1, n, settle, 0)
    local.wait()


def expert_all_to_all(x, collective_id):
    n = x.shape[0]
    return pl.pallas_call(
        _a2a_kernel,
        out_shape=jax.ShapeDtypeStruct(x.shape, x.dtype),
        in_specs=[pl.BlockSpec(memory_space=pl.ANY)],
        out_specs=pl.BlockSpec(memory_space=pl.ANY),
        scratch_shapes=[
            pltpu.SemaphoreType.DMA((n,)),
            pltpu.SemaphoreType.DMA((n,)),
            pltpu.SemaphoreType.DMA(()),
        ],
        compiler_params=pltpu.CompilerParams(collective_id=collective_id, has_side_effects=True),
        cost_estimate=pl.CostEstimate(
            flops=0, transcendentals=0, bytes_accessed=2 * x.size * x.dtype.itemsize
        ),
    )(x)


def expert_chunk(rows, scaled, w_in, w_out, quarter, ids):
    slots = rows.shape[2]
    send = jnp.concatenate([rows, scaled], axis=2)
    arrived = expert_all_to_all(send.reshape(send.shape[0], -1, quarter), ids[0]).reshape(send.shape)
    whole = lax.all_gather(arrived, "tensor", axis=3, tiled=True)
    expert_rows = whole[:, :, :slots]
    expert_scaled = whole[:, :, slots:]
    preact = jnp.einsum("nesd,edh->nesh", expert_rows, w_in, preferred_element_type=jnp.float32)
    sigmoid_val = jax.nn.sigmoid(preact)
    hidden = (preact * sigmoid_val).astype(jnp.bfloat16)
    out_part = jnp.einsum("nesh,ehd->nesd", hidden, w_out, preferred_element_type=jnp.float32)
    grad_hidden = jnp.einsum(
        "nesd,ehd->nesh", expert_scaled, w_out, preferred_element_type=jnp.float32
    )
    grad_preact = (grad_hidden * sigmoid_val * (1.0 + preact * (1.0 - sigmoid_val))).astype(
        jnp.bfloat16
    )
    d_w_out = jnp.einsum(
        "nesh,nesd->ehd", hidden, expert_scaled, preferred_element_type=jnp.float32
    )
    d_w_in = jnp.einsum(
        "nesd,nesh->edh", expert_rows, grad_preact, preferred_element_type=jnp.float32
    )
    grad_part = jnp.einsum("nesh,edh->nesd", grad_preact, w_in, preferred_element_type=jnp.float32)
    parts = jnp.concatenate(
        [out_part.astype(jnp.bfloat16), grad_part.astype(jnp.bfloat16)], axis=2
    )
    sums = lax.psum_scatter(parts, "tensor", scatter_dimension=3, tiled=True)
    back = expert_all_to_all(sums.reshape(sums.shape[0], -1, quarter), ids[1]).reshape(sums.shape)
    return back[:, :, :slots], back[:, :, slots:], d_w_in, d_w_out


def shards(tokens, cotangent, routing, gates, w_in, w_out):
    devices = lax.axis_size("expert")
    local_experts = w_in.shape[0]
    experts = devices * local_experts
    tok_rows = routing.shape[0]
    capacity = tok_rows // 4
    buffer_rows = experts * capacity
    highest = lax.Precision.HIGHEST
    matches = (routing[:, :, None] == jnp.arange(experts, dtype=jnp.int32)[None, None, :]).astype(
        jnp.int32
    )
    per_token = jnp.sum(matches, axis=1)
    earlier = jnp.cumsum(per_token, axis=0) - per_token
    destination = routing * capacity + jnp.take_along_axis(earlier, routing, axis=1)
    placed = (
        destination[:, :, None] == jnp.arange(buffer_rows, dtype=jnp.int32)[None, None, :]
    ).astype(jnp.float32)
    membership = jnp.sum(placed, axis=1)
    weighting = jnp.sum(placed * gates[:, :, None], axis=1)
    quarter = tokens.shape[1]
    rows = jnp.einsum(
        "tr,td->rd",
        membership.astype(jnp.bfloat16),
        tokens,
        preferred_element_type=jnp.float32,
    ).astype(jnp.bfloat16)
    scaled = jnp.einsum(
        "tr,td->rd", weighting, cotangent.astype(jnp.float32), precision=highest
    ).astype(jnp.bfloat16)
    rows = rows.reshape(devices, local_experts, capacity, quarter)
    scaled = scaled.reshape(devices, local_experts, capacity, quarter)
    step = capacity // CHUNKS
    back_out, back_grad, d_w_in, d_w_out = [], [], None, None
    for c in range(CHUNKS):
        window = slice(c * step, (c + 1) * step)
        with jax.named_scope(f"slot_chunk{c}"):
            b_out, b_grad, g_in, g_out = expert_chunk(
                rows[:, :, window], scaled[:, :, window], w_in, w_out, quarter, (2 * c, 2 * c + 1)
            )
        back_out.append(b_out)
        back_grad.append(b_grad)
        d_w_in = g_in if d_w_in is None else d_w_in + g_in
        d_w_out = g_out if d_w_out is None else d_w_out + g_out
    back_out = jnp.concatenate(back_out, axis=2).reshape(buffer_rows, quarter).astype(jnp.float32)
    back_grad = jnp.concatenate(back_grad, axis=2).reshape(buffer_rows, quarter).astype(jnp.float32)
    mixed = jnp.einsum("tr,rd->td", weighting, back_out, precision=highest).astype(jnp.bfloat16)
    d_tokens = jnp.einsum("tr,rd->td", membership, back_grad, precision=highest).astype(
        jnp.bfloat16
    )
    return (mixed, d_tokens, d_w_in.astype(jnp.bfloat16), d_w_out.astype(jnp.bfloat16))


def solution(mesh):
    placed = (
        P("expert", "tensor"),
        P("expert", "tensor"),
        P("expert", None),
        P("expert", None),
        P("expert", None, "tensor"),
        P("expert", "tensor", None),
    )
    return jax.shard_map(
        shards,
        mesh=mesh,
        in_specs=placed,
        out_specs=(
            P("expert", "tensor"),
            P("expert", "tensor"),
            P("expert", None, "tensor"),
            P("expert", "tensor", None),
        ),
        check_vma=False,
    )
```

```python
import jax
import jax.numpy as jnp
from jax import lax
from jax.experimental import pallas as pl
from jax.experimental.pallas import tpu as pltpu
from jax.sharding import PartitionSpec as P

CHUNKS = 2


def _a2a_kernel(x_ref, o_ref, send_sem, recv_sem, local_sem):
    n = x_ref.shape[0]
    me = lax.axis_index("expert")
    tau = lax.axis_index("tensor")
    barrier = pltpu.get_barrier_semaphore()

    def greet(k, carry):
        peer = lax.rem(me + k, n)
        pl.semaphore_signal(
            barrier, inc=1, device_id=(peer, tau), device_id_type=pl.DeviceIdType.MESH
        )
        return carry

    lax.fori_loop(1, n, greet, 0)
    pl.semaphore_wait(barrier, n - 1)

    local = pltpu.make_async_copy(x_ref.at[me], o_ref.at[me], local_sem)
    local.start()

    def push(k, carry):
        peer = lax.rem(me + k, n)
        pltpu.make_async_remote_copy(
            src_ref=x_ref.at[peer],
            dst_ref=o_ref.at[me],
            send_sem=send_sem.at[k],
            recv_sem=recv_sem.at[k],
            device_id=(peer, tau),
            device_id_type=pl.DeviceIdType.MESH,
        ).start()
        return carry

    lax.fori_loop(1, n, push, 0)

    def settle(k, carry):
        peer = lax.rem(me + k, n)
        source = lax.rem(me + n - k, n)
        pltpu.make_async_remote_copy(
            src_ref=x_ref.at[peer],
            dst_ref=o_ref.at[source],
            send_sem=send_sem.at[k],
            recv_sem=recv_sem.at[k],
            device_id=(peer, tau),
            device_id_type=pl.DeviceIdType.MESH,
        ).wait()
        return carry

    lax.fori_loop(1, n, settle, 0)
    local.wait()


def expert_all_to_all(x, collective_id):
    n = x.shape[0]
    return pl.pallas_call(
        _a2a_kernel,
        out_shape=jax.ShapeDtypeStruct(x.shape, x.dtype),
        in_specs=[pl.BlockSpec(memory_space=pl.ANY)],
        out_specs=pl.BlockSpec(memory_space=pl.ANY),
        scratch_shapes=[
            pltpu.SemaphoreType.DMA((n,)),
            pltpu.SemaphoreType.DMA((n,)),
            pltpu.SemaphoreType.DMA(()),
        ],
        compiler_params=pltpu.CompilerParams(collective_id=collective_id, has_side_effects=True),
        cost_estimate=pl.CostEstimate(
            flops=0, transcendentals=0, bytes_accessed=2 * x.size * x.dtype.itemsize
        ),
    )(x)


def _dispatch_kernel(x_ref, o_ref, xz_send, xz_recv, y_send, y_recv, local_sem):
    n = x_ref.shape[0]
    groups = o_ref.shape[1]
    me = lax.axis_index("expert")
    tau = lax.axis_index("tensor")
    barrier = pltpu.get_barrier_semaphore()

    def greet(k, carry):
        pl.semaphore_signal(
            barrier, inc=1, device_id=(lax.rem(me + k, n), tau), device_id_type=pl.DeviceIdType.MESH
        )
        return carry

    lax.fori_loop(1, n, greet, 0)
    for j in range(1, groups):
        pl.semaphore_signal(
            barrier, inc=1, device_id=(me, lax.rem(tau + j, groups)), device_id_type=pl.DeviceIdType.MESH
        )
    pl.semaphore_wait(barrier, n - 1 + groups - 1)

    local = pltpu.make_async_copy(x_ref.at[me], o_ref.at[me, tau], local_sem)
    local.start()

    def xz_copy(k):
        peer = lax.rem(me + k, n)
        return pltpu.make_async_remote_copy(
            src_ref=x_ref.at[peer],
            dst_ref=o_ref.at[me, tau],
            send_sem=xz_send.at[k],
            recv_sem=xz_recv.at[k],
            device_id=(peer, tau),
            device_id_type=pl.DeviceIdType.MESH,
        )

    def xz_arrival(k):
        peer = lax.rem(me + k, n)
        source = lax.rem(me + n - k, n)
        return pltpu.make_async_remote_copy(
            src_ref=x_ref.at[peer],
            dst_ref=o_ref.at[source, tau],
            send_sem=xz_send.at[k],
            recv_sem=xz_recv.at[k],
            device_id=(peer, tau),
            device_id_type=pl.DeviceIdType.MESH,
        )

    def y_copy(j, k):
        source = lax.rem(me + n - k, n)
        return pltpu.make_async_remote_copy(
            src_ref=o_ref.at[source, tau],
            dst_ref=o_ref.at[source, tau],
            send_sem=y_send.at[j - 1, k],
            recv_sem=y_recv.at[j - 1, k],
            device_id=(me, lax.rem(tau + j, groups)),
            device_id_type=pl.DeviceIdType.MESH,
        )

    def y_arrival(j, k):
        source = lax.rem(me + n - k, n)
        return pltpu.make_async_remote_copy(
            src_ref=o_ref.at[source, tau],
            dst_ref=o_ref.at[source, lax.rem(tau + groups - j, groups)],
            send_sem=y_send.at[j - 1, k],
            recv_sem=y_recv.at[j - 1, k],
            device_id=(me, lax.rem(tau + j, groups)),
            device_id_type=pl.DeviceIdType.MESH,
        )

    def push(k, carry):
        xz_copy(k).start()
        return carry

    lax.fori_loop(1, n, push, 0)

    local.wait()
    for j in range(1, groups):
        y_copy(j, 0).start()

    def forward(k, carry):
        xz_arrival(k).wait_recv()
        for j in range(1, groups):
            y_copy(j, k).start()
        return carry

    lax.fori_loop(1, n, forward, 0)

    def settle(k, carry):
        xz_copy(k).wait_send()
        return carry

    lax.fori_loop(1, n, settle, 0)

    def settle_y(k, carry):
        for j in range(1, groups):
            y_copy(j, k).wait_send()
            y_arrival(j, k).wait_recv()
        return carry

    lax.fori_loop(0, n, settle_y, 0)


def dispatch(x, groups, collective_id):
    n, rows, width = x.shape
    return pl.pallas_call(
        _dispatch_kernel,
        out_shape=jax.ShapeDtypeStruct((n, groups, rows, width), x.dtype),
        in_specs=[pl.BlockSpec(memory_space=pl.ANY)],
        out_specs=pl.BlockSpec(memory_space=pl.ANY),
        scratch_shapes=[
            pltpu.SemaphoreType.DMA((n,)),
            pltpu.SemaphoreType.DMA((n,)),
            pltpu.SemaphoreType.DMA((groups - 1, n)),
            pltpu.SemaphoreType.DMA((groups - 1, n)),
            pltpu.SemaphoreType.DMA(()),
        ],
        compiler_params=pltpu.CompilerParams(collective_id=collective_id, has_side_effects=True),
        cost_estimate=pl.CostEstimate(
            flops=0, transcendentals=0, bytes_accessed=(1 + 2 * groups) * x.size * x.dtype.itemsize
        ),
    )(x)


def expert_chunk(rows, scaled, w_in, w_out, quarter, ids):
    slots = rows.shape[2]
    send = jnp.concatenate([rows, scaled], axis=2)
    groups = lax.axis_size("tensor")
    spread = dispatch(send.reshape(send.shape[0], -1, quarter), groups, ids[0])
    whole = jnp.swapaxes(spread, 1, 2).reshape(send.shape[:3] + (groups * quarter,))
    expert_rows = whole[:, :, :slots]
    expert_scaled = whole[:, :, slots:]
    preact = jnp.einsum("nesd,edh->nesh", expert_rows, w_in, preferred_element_type=jnp.float32)
    sigmoid_val = jax.nn.sigmoid(preact)
    hidden = (preact * sigmoid_val).astype(jnp.bfloat16)
    out_part = jnp.einsum("nesh,ehd->nesd", hidden, w_out, preferred_element_type=jnp.float32)
    grad_hidden = jnp.einsum(
        "nesd,ehd->nesh", expert_scaled, w_out, preferred_element_type=jnp.float32
    )
    grad_preact = (grad_hidden * sigmoid_val * (1.0 + preact * (1.0 - sigmoid_val))).astype(
        jnp.bfloat16
    )
    d_w_out = jnp.einsum(
        "nesh,nesd->ehd", hidden, expert_scaled, preferred_element_type=jnp.float32
    )
    d_w_in = jnp.einsum(
        "nesd,nesh->edh", expert_rows, grad_preact, preferred_element_type=jnp.float32
    )
    grad_part = jnp.einsum("nesh,edh->nesd", grad_preact, w_in, preferred_element_type=jnp.float32)
    parts = jnp.concatenate(
        [out_part.astype(jnp.bfloat16), grad_part.astype(jnp.bfloat16)], axis=2
    )
    sums = lax.psum_scatter(parts, "tensor", scatter_dimension=3, tiled=True)
    back = expert_all_to_all(sums.reshape(sums.shape[0], -1, quarter), ids[1]).reshape(sums.shape)
    return back[:, :, :slots], back[:, :, slots:], d_w_in, d_w_out


def shards(tokens, cotangent, routing, gates, w_in, w_out):
    devices = lax.axis_size("expert")
    local_experts = w_in.shape[0]
    experts = devices * local_experts
    tok_rows = routing.shape[0]
    capacity = tok_rows // 4
    buffer_rows = experts * capacity
    highest = lax.Precision.HIGHEST
    matches = (routing[:, :, None] == jnp.arange(experts, dtype=jnp.int32)[None, None, :]).astype(
        jnp.int32
    )
    per_token = jnp.sum(matches, axis=1)
    earlier = jnp.cumsum(per_token, axis=0) - per_token
    destination = routing * capacity + jnp.take_along_axis(earlier, routing, axis=1)
    placed = (
        destination[:, :, None] == jnp.arange(buffer_rows, dtype=jnp.int32)[None, None, :]
    ).astype(jnp.float32)
    membership = jnp.sum(placed, axis=1)
    weighting = jnp.sum(placed * gates[:, :, None], axis=1)
    quarter = tokens.shape[1]
    rows = jnp.einsum(
        "tr,td->rd",
        membership.astype(jnp.bfloat16),
        tokens,
        preferred_element_type=jnp.float32,
    ).astype(jnp.bfloat16)
    scaled = jnp.einsum(
        "tr,td->rd", weighting, cotangent.astype(jnp.float32), precision=highest
    ).astype(jnp.bfloat16)
    rows = rows.reshape(devices, local_experts, capacity, quarter)
    scaled = scaled.reshape(devices, local_experts, capacity, quarter)
    step = capacity // CHUNKS
    back_out, back_grad, d_w_in, d_w_out = [], [], None, None
    for c in range(CHUNKS):
        window = slice(c * step, (c + 1) * step)
        with jax.named_scope(f"slot_chunk{c}"):
            b_out, b_grad, g_in, g_out = expert_chunk(
                rows[:, :, window], scaled[:, :, window], w_in, w_out, quarter, (2 * c, 2 * c + 1)
            )
        back_out.append(b_out)
        back_grad.append(b_grad)
        d_w_in = g_in if d_w_in is None else d_w_in + g_in
        d_w_out = g_out if d_w_out is None else d_w_out + g_out
    back_out = jnp.concatenate(back_out, axis=2).reshape(buffer_rows, quarter).astype(jnp.float32)
    back_grad = jnp.concatenate(back_grad, axis=2).reshape(buffer_rows, quarter).astype(jnp.float32)
    mixed = jnp.einsum("tr,rd->td", weighting, back_out, precision=highest).astype(jnp.bfloat16)
    d_tokens = jnp.einsum("tr,rd->td", membership, back_grad, precision=highest).astype(
        jnp.bfloat16
    )
    return (mixed, d_tokens, d_w_in.astype(jnp.bfloat16), d_w_out.astype(jnp.bfloat16))


def solution(mesh):
    placed = (
        P("expert", "tensor"),
        P("expert", "tensor"),
        P("expert", None),
        P("expert", None),
        P("expert", None, "tensor"),
        P("expert", "tensor", None),
    )
    return jax.shard_map(
        shards,
        mesh=mesh,
        in_specs=placed,
        out_specs=(
            P("expert", "tensor"),
            P("expert", "tensor"),
            P("expert", None, "tensor"),
            P("expert", "tensor", None),
        ),
        check_vma=False,
    )
```

```python
import jax
import jax.numpy as jnp
from jax import lax
from jax.experimental import pallas as pl
from jax.experimental.pallas import tpu as pltpu
from jax.sharding import PartitionSpec as P

CHUNKS = 2


def _a2a_kernel(x_ref, o_ref, send_sem, recv_sem, local_sem):
    n = x_ref.shape[0]
    me = lax.axis_index("expert")
    tau = lax.axis_index("tensor")
    barrier = pltpu.get_barrier_semaphore()

    def greet(k, carry):
        peer = lax.rem(me + k, n)
        pl.semaphore_signal(
            barrier, inc=1, device_id=(peer, tau), device_id_type=pl.DeviceIdType.MESH
        )
        return carry

    lax.fori_loop(1, n, greet, 0)
    pl.semaphore_wait(barrier, n - 1)

    local = pltpu.make_async_copy(x_ref.at[me], o_ref.at[me], local_sem)
    local.start()

    def push(k, carry):
        peer = lax.rem(me + k, n)
        pltpu.make_async_remote_copy(
            src_ref=x_ref.at[peer],
            dst_ref=o_ref.at[me],
            send_sem=send_sem.at[k],
            recv_sem=recv_sem.at[k],
            device_id=(peer, tau),
            device_id_type=pl.DeviceIdType.MESH,
        ).start()
        return carry

    lax.fori_loop(1, n, push, 0)

    def settle(k, carry):
        peer = lax.rem(me + k, n)
        source = lax.rem(me + n - k, n)
        pltpu.make_async_remote_copy(
            src_ref=x_ref.at[peer],
            dst_ref=o_ref.at[source],
            send_sem=send_sem.at[k],
            recv_sem=recv_sem.at[k],
            device_id=(peer, tau),
            device_id_type=pl.DeviceIdType.MESH,
        ).wait()
        return carry

    lax.fori_loop(1, n, settle, 0)
    local.wait()


def expert_all_to_all(x, collective_id):
    n = x.shape[0]
    return pl.pallas_call(
        _a2a_kernel,
        out_shape=jax.ShapeDtypeStruct(x.shape, x.dtype),
        in_specs=[pl.BlockSpec(memory_space=pl.ANY)],
        out_specs=pl.BlockSpec(memory_space=pl.ANY),
        scratch_shapes=[
            pltpu.SemaphoreType.DMA((n,)),
            pltpu.SemaphoreType.DMA((n,)),
            pltpu.SemaphoreType.DMA(()),
        ],
        compiler_params=pltpu.CompilerParams(collective_id=collective_id, has_side_effects=True),
        cost_estimate=pl.CostEstimate(
            flops=0, transcendentals=0, bytes_accessed=2 * x.size * x.dtype.itemsize
        ),
    )(x)


def _dispatch_kernel(x_ref, o_ref, xz_send, xz_recv, y_send, y_recv, local_sem):
    n = x_ref.shape[0]
    groups = o_ref.shape[1]
    me = lax.axis_index("expert")
    tau = lax.axis_index("tensor")
    barrier = pltpu.get_barrier_semaphore()

    def greet(k, carry):
        pl.semaphore_signal(
            barrier, inc=1, device_id=(lax.rem(me + k, n), tau), device_id_type=pl.DeviceIdType.MESH
        )
        return carry

    lax.fori_loop(1, n, greet, 0)
    for j in range(1, groups):
        pl.semaphore_signal(
            barrier, inc=1, device_id=(me, lax.rem(tau + j, groups)), device_id_type=pl.DeviceIdType.MESH
        )
    pl.semaphore_wait(barrier, n - 1 + groups - 1)

    local = pltpu.make_async_copy(x_ref.at[me], o_ref.at[me, tau], local_sem)
    local.start()

    def xz_copy(k):
        peer = lax.rem(me + k, n)
        return pltpu.make_async_remote_copy(
            src_ref=x_ref.at[peer],
            dst_ref=o_ref.at[me, tau],
            send_sem=xz_send.at[k],
            recv_sem=xz_recv.at[k],
            device_id=(peer, tau),
            device_id_type=pl.DeviceIdType.MESH,
        )

    def xz_arrival(k):
        peer = lax.rem(me + k, n)
        source = lax.rem(me + n - k, n)
        return pltpu.make_async_remote_copy(
            src_ref=x_ref.at[peer],
            dst_ref=o_ref.at[source, tau],
            send_sem=xz_send.at[k],
            recv_sem=xz_recv.at[k],
            device_id=(peer, tau),
            device_id_type=pl.DeviceIdType.MESH,
        )

    def y_copy(j, k):
        source = lax.rem(me + n - k, n)
        return pltpu.make_async_remote_copy(
            src_ref=o_ref.at[source, tau],
            dst_ref=o_ref.at[source, tau],
            send_sem=y_send.at[j - 1, k],
            recv_sem=y_recv.at[j - 1, k],
            device_id=(me, lax.rem(tau + j, groups)),
            device_id_type=pl.DeviceIdType.MESH,
        )

    def y_arrival(j, k):
        source = lax.rem(me + n - k, n)
        return pltpu.make_async_remote_copy(
            src_ref=o_ref.at[source, tau],
            dst_ref=o_ref.at[source, lax.rem(tau + groups - j, groups)],
            send_sem=y_send.at[j - 1, k],
            recv_sem=y_recv.at[j - 1, k],
            device_id=(me, lax.rem(tau + j, groups)),
            device_id_type=pl.DeviceIdType.MESH,
        )

    def push(k, carry):
        xz_copy(k).start()
        return carry

    lax.fori_loop(1, n, push, 0)

    local.wait()
    for j in range(1, groups):
        y_copy(j, 0).start()

    def forward(k, carry):
        xz_arrival(k).wait_recv()
        for j in range(1, groups):
            y_copy(j, k).start()
        return carry

    lax.fori_loop(1, n, forward, 0)

    def settle(k, carry):
        xz_copy(k).wait_send()
        return carry

    lax.fori_loop(1, n, settle, 0)

    def settle_y(k, carry):
        for j in range(1, groups):
            y_copy(j, k).wait_send()
            y_arrival(j, k).wait_recv()
        return carry

    lax.fori_loop(0, n, settle_y, 0)


def dispatch(x, groups, collective_id):
    n, rows, width = x.shape
    return pl.pallas_call(
        _dispatch_kernel,
        out_shape=jax.ShapeDtypeStruct((n, groups, rows, width), x.dtype),
        in_specs=[pl.BlockSpec(memory_space=pl.ANY)],
        out_specs=pl.BlockSpec(memory_space=pl.ANY),
        scratch_shapes=[
            pltpu.SemaphoreType.DMA((n,)),
            pltpu.SemaphoreType.DMA((n,)),
            pltpu.SemaphoreType.DMA((groups - 1, n)),
            pltpu.SemaphoreType.DMA((groups - 1, n)),
            pltpu.SemaphoreType.DMA(()),
        ],
        compiler_params=pltpu.CompilerParams(collective_id=collective_id, has_side_effects=True),
        cost_estimate=pl.CostEstimate(
            flops=0, transcendentals=0, bytes_accessed=(1 + 2 * groups) * x.size * x.dtype.itemsize
        ),
    )(x)


def expert_chunk(expert_rows, expert_scaled, w_in, w_out, quarter, collective_id):
    slots = expert_rows.shape[2]
    preact = jnp.einsum("nesd,edh->nesh", expert_rows, w_in, preferred_element_type=jnp.float32)
    sigmoid_val = jax.nn.sigmoid(preact)
    hidden = (preact * sigmoid_val).astype(jnp.bfloat16)
    out_part = jnp.einsum("nesh,ehd->nesd", hidden, w_out, preferred_element_type=jnp.float32)
    grad_hidden = jnp.einsum(
        "nesd,ehd->nesh", expert_scaled, w_out, preferred_element_type=jnp.float32
    )
    grad_preact = (grad_hidden * sigmoid_val * (1.0 + preact * (1.0 - sigmoid_val))).astype(
        jnp.bfloat16
    )
    d_w_out = jnp.einsum(
        "nesh,nesd->ehd", hidden, expert_scaled, preferred_element_type=jnp.float32
    )
    d_w_in = jnp.einsum(
        "nesd,nesh->edh", expert_rows, grad_preact, preferred_element_type=jnp.float32
    )
    grad_part = jnp.einsum("nesh,edh->nesd", grad_preact, w_in, preferred_element_type=jnp.float32)
    parts = jnp.concatenate(
        [out_part.astype(jnp.bfloat16), grad_part.astype(jnp.bfloat16)], axis=2
    )
    sums = lax.psum_scatter(parts, "tensor", scatter_dimension=3, tiled=True)
    back = expert_all_to_all(sums.reshape(sums.shape[0], -1, quarter), collective_id).reshape(sums.shape)
    return back[:, :, :slots], back[:, :, slots:], d_w_in, d_w_out


def shards(tokens, cotangent, routing, gates, w_in, w_out):
    devices = lax.axis_size("expert")
    groups = lax.axis_size("tensor")
    local_experts = w_in.shape[0]
    experts = devices * local_experts
    tok_rows = routing.shape[0]
    capacity = tok_rows // 4
    buffer_rows = experts * capacity
    highest = lax.Precision.HIGHEST
    matches = (routing[:, :, None] == jnp.arange(experts, dtype=jnp.int32)[None, None, :]).astype(
        jnp.int32
    )
    per_token = jnp.sum(matches, axis=1)
    earlier = jnp.cumsum(per_token, axis=0) - per_token
    destination = routing * capacity + jnp.take_along_axis(earlier, routing, axis=1)
    placed = (
        destination[:, :, None] == jnp.arange(buffer_rows, dtype=jnp.int32)[None, None, :]
    ).astype(jnp.float32)
    membership = jnp.sum(placed, axis=1)
    weighting = jnp.sum(placed * gates[:, :, None], axis=1)
    quarter = tokens.shape[1]
    rows = jnp.einsum(
        "tr,td->rd",
        membership.astype(jnp.bfloat16),
        tokens,
        preferred_element_type=jnp.float32,
    ).astype(jnp.bfloat16)
    scaled = jnp.einsum(
        "tr,td->rd", weighting, cotangent.astype(jnp.float32), precision=highest
    ).astype(jnp.bfloat16)
    send = jnp.concatenate(
        [
            rows.reshape(devices, local_experts * capacity, quarter),
            scaled.reshape(devices, local_experts * capacity, quarter),
        ],
        axis=1,
    )
    spread = dispatch(send, groups, 0)
    whole = jnp.swapaxes(spread, 1, 2).reshape(devices, 2, local_experts, capacity, groups * quarter)
    step = capacity // CHUNKS
    back_out, back_grad, d_w_in, d_w_out = [], [], None, None
    for c in range(CHUNKS):
        window = slice(c * step, (c + 1) * step)
        with jax.named_scope(f"slot_chunk{c}"):
            b_out, b_grad, g_in, g_out = expert_chunk(
                whole[:, 0, :, window], whole[:, 1, :, window], w_in, w_out, quarter, 1 + c
            )
        back_out.append(b_out)
        back_grad.append(b_grad)
        d_w_in = g_in if d_w_in is None else d_w_in + g_in
        d_w_out = g_out if d_w_out is None else d_w_out + g_out
    back_out = jnp.concatenate(back_out, axis=2).reshape(buffer_rows, quarter).astype(jnp.float32)
    back_grad = jnp.concatenate(back_grad, axis=2).reshape(buffer_rows, quarter).astype(jnp.float32)
    mixed = jnp.einsum("tr,rd->td", weighting, back_out, precision=highest).astype(jnp.bfloat16)
    d_tokens = jnp.einsum("tr,rd->td", membership, back_grad, precision=highest).astype(
        jnp.bfloat16
    )
    return (mixed, d_tokens, d_w_in.astype(jnp.bfloat16), d_w_out.astype(jnp.bfloat16))


def solution(mesh):
    placed = (
        P("expert", "tensor"),
        P("expert", "tensor"),
        P("expert", None),
        P("expert", None),
        P("expert", None, "tensor"),
        P("expert", "tensor", None),
    )
    return jax.shard_map(
        shards,
        mesh=mesh,
        in_specs=placed,
        out_specs=(
            P("expert", "tensor"),
            P("expert", "tensor"),
            P("expert", None, "tensor"),
            P("expert", "tensor", None),
        ),
        check_vma=False,
    )
```

```python
import jax
import jax.numpy as jnp
from jax import lax
from jax.experimental import pallas as pl
from jax.experimental.pallas import tpu as pltpu
from jax.sharding import PartitionSpec as P

CHUNKS = 2


def _a2a_kernel(x_ref, o_ref, send_sem, recv_sem, local_sem):
    n = x_ref.shape[0]
    me = lax.axis_index("expert")
    tau = lax.axis_index("tensor")
    barrier = pltpu.get_barrier_semaphore()

    def greet(k, carry):
        peer = lax.rem(me + k, n)
        pl.semaphore_signal(
            barrier, inc=1, device_id=(peer, tau), device_id_type=pl.DeviceIdType.MESH
        )
        return carry

    lax.fori_loop(1, n, greet, 0)
    pl.semaphore_wait(barrier, n - 1)

    local = pltpu.make_async_copy(x_ref.at[me], o_ref.at[me], local_sem)
    local.start()

    def push(k, carry):
        peer = lax.rem(me + k, n)
        pltpu.make_async_remote_copy(
            src_ref=x_ref.at[peer],
            dst_ref=o_ref.at[me],
            send_sem=send_sem.at[k],
            recv_sem=recv_sem.at[k],
            device_id=(peer, tau),
            device_id_type=pl.DeviceIdType.MESH,
        ).start()
        return carry

    lax.fori_loop(1, n, push, 0)

    def settle(k, carry):
        peer = lax.rem(me + k, n)
        source = lax.rem(me + n - k, n)
        pltpu.make_async_remote_copy(
            src_ref=x_ref.at[peer],
            dst_ref=o_ref.at[source],
            send_sem=send_sem.at[k],
            recv_sem=recv_sem.at[k],
            device_id=(peer, tau),
            device_id_type=pl.DeviceIdType.MESH,
        ).wait()
        return carry

    lax.fori_loop(1, n, settle, 0)
    local.wait()


def expert_all_to_all(x, collective_id):
    n = x.shape[0]
    return pl.pallas_call(
        _a2a_kernel,
        out_shape=jax.ShapeDtypeStruct(x.shape, x.dtype),
        in_specs=[pl.BlockSpec(memory_space=pl.ANY)],
        out_specs=pl.BlockSpec(memory_space=pl.ANY),
        scratch_shapes=[
            pltpu.SemaphoreType.DMA((n,)),
            pltpu.SemaphoreType.DMA((n,)),
            pltpu.SemaphoreType.DMA(()),
        ],
        compiler_params=pltpu.CompilerParams(collective_id=collective_id, has_side_effects=True),
        cost_estimate=pl.CostEstimate(
            flops=0, transcendentals=0, bytes_accessed=2 * x.size * x.dtype.itemsize
        ),
    )(x)


def _dispatch_kernel(x_ref, o_ref, xz_send, xz_recv, y_send, y_recv, local_sem):
    n, rows, width = x_ref.shape
    groups = o_ref.shape[2] // width
    me = lax.axis_index("expert")
    tau = lax.axis_index("tensor")
    barrier = pltpu.get_barrier_semaphore()

    def cols(g):
        return pl.ds(pl.multiple_of(g * width, 128), width)

    def greet(k, carry):
        pl.semaphore_signal(
            barrier, inc=1, device_id=(lax.rem(me + k, n), tau), device_id_type=pl.DeviceIdType.MESH
        )
        return carry

    lax.fori_loop(1, n, greet, 0)
    for j in range(1, groups):
        pl.semaphore_signal(
            barrier, inc=1, device_id=(me, lax.rem(tau + j, groups)), device_id_type=pl.DeviceIdType.MESH
        )
    pl.semaphore_wait(barrier, n - 1 + groups - 1)

    local = pltpu.make_async_copy(x_ref.at[me], o_ref.at[me, :, cols(tau)], local_sem)
    local.start()

    def xz_copy(k):
        peer = lax.rem(me + k, n)
        return pltpu.make_async_remote_copy(
            src_ref=x_ref.at[peer],
            dst_ref=o_ref.at[me, :, cols(tau)],
            send_sem=xz_send.at[k],
            recv_sem=xz_recv.at[k],
            device_id=(peer, tau),
            device_id_type=pl.DeviceIdType.MESH,
        )

    def xz_arrival(k):
        peer = lax.rem(me + k, n)
        source = lax.rem(me + n - k, n)
        return pltpu.make_async_remote_copy(
            src_ref=x_ref.at[peer],
            dst_ref=o_ref.at[source, :, cols(tau)],
            send_sem=xz_send.at[k],
            recv_sem=xz_recv.at[k],
            device_id=(peer, tau),
            device_id_type=pl.DeviceIdType.MESH,
        )

    def y_copy(j, k):
        source = lax.rem(me + n - k, n)
        return pltpu.make_async_remote_copy(
            src_ref=o_ref.at[source, :, cols(tau)],
            dst_ref=o_ref.at[source, :, cols(tau)],
            send_sem=y_send.at[j - 1, k],
            recv_sem=y_recv.at[j - 1, k],
            device_id=(me, lax.rem(tau + j, groups)),
            device_id_type=pl.DeviceIdType.MESH,
        )

    def y_arrival(j, k):
        source = lax.rem(me + n - k, n)
        return pltpu.make_async_remote_copy(
            src_ref=o_ref.at[source, :, cols(tau)],
            dst_ref=o_ref.at[source, :, cols(lax.rem(tau + groups - j, groups))],
            send_sem=y_send.at[j - 1, k],
            recv_sem=y_recv.at[j - 1, k],
            device_id=(me, lax.rem(tau + j, groups)),
            device_id_type=pl.DeviceIdType.MESH,
        )

    def push(k, carry):
        xz_copy(k).start()
        return carry

    lax.fori_loop(1, n, push, 0)

    local.wait()
    for j in range(1, groups):
        y_copy(j, 0).start()

    def forward(k, carry):
        xz_arrival(k).wait_recv()
        for j in range(1, groups):
            y_copy(j, k).start()
        return carry

    lax.fori_loop(1, n, forward, 0)

    def settle(k, carry):
        xz_copy(k).wait_send()
        return carry

    lax.fori_loop(1, n, settle, 0)

    def settle_y(k, carry):
        for j in range(1, groups):
            y_copy(j, k).wait_send()
            y_arrival(j, k).wait_recv()
        return carry

    lax.fori_loop(0, n, settle_y, 0)


def dispatch(x, groups, collective_id):
    n, rows, width = x.shape
    return pl.pallas_call(
        _dispatch_kernel,
        out_shape=jax.ShapeDtypeStruct((n, rows, groups * width), x.dtype),
        in_specs=[pl.BlockSpec(memory_space=pl.ANY)],
        out_specs=pl.BlockSpec(memory_space=pl.ANY),
        scratch_shapes=[
            pltpu.SemaphoreType.DMA((n,)),
            pltpu.SemaphoreType.DMA((n,)),
            pltpu.SemaphoreType.DMA((groups - 1, n)),
            pltpu.SemaphoreType.DMA((groups - 1, n)),
            pltpu.SemaphoreType.DMA(()),
        ],
        compiler_params=pltpu.CompilerParams(collective_id=collective_id, has_side_effects=True),
        cost_estimate=pl.CostEstimate(
            flops=0, transcendentals=0, bytes_accessed=(1 + 2 * groups) * x.size * x.dtype.itemsize
        ),
    )(x)


def expert_chunk(expert_rows, expert_scaled, w_in, w_out, quarter, collective_id):
    slots = expert_rows.shape[2]
    preact = jnp.einsum("nesd,edh->nesh", expert_rows, w_in, preferred_element_type=jnp.float32)
    sigmoid_val = jax.nn.sigmoid(preact)
    hidden = (preact * sigmoid_val).astype(jnp.bfloat16)
    out_part = jnp.einsum("nesh,ehd->nesd", hidden, w_out, preferred_element_type=jnp.float32)
    grad_hidden = jnp.einsum(
        "nesd,ehd->nesh", expert_scaled, w_out, preferred_element_type=jnp.float32
    )
    grad_preact = (grad_hidden * sigmoid_val * (1.0 + preact * (1.0 - sigmoid_val))).astype(
        jnp.bfloat16
    )
    d_w_out = jnp.einsum(
        "nesh,nesd->ehd", hidden, expert_scaled, preferred_element_type=jnp.float32
    )
    d_w_in = jnp.einsum(
        "nesd,nesh->edh", expert_rows, grad_preact, preferred_element_type=jnp.float32
    )
    grad_part = jnp.einsum("nesh,edh->nesd", grad_preact, w_in, preferred_element_type=jnp.float32)
    parts = jnp.concatenate(
        [out_part.astype(jnp.bfloat16), grad_part.astype(jnp.bfloat16)], axis=2
    )
    sums = lax.psum_scatter(parts, "tensor", scatter_dimension=3, tiled=True)
    back = expert_all_to_all(sums.reshape(sums.shape[0], -1, quarter), collective_id).reshape(sums.shape)
    return back[:, :, :slots], back[:, :, slots:], d_w_in, d_w_out


def shards(tokens, cotangent, routing, gates, w_in, w_out):
    devices = lax.axis_size("expert")
    groups = lax.axis_size("tensor")
    local_experts = w_in.shape[0]
    experts = devices * local_experts
    tok_rows = routing.shape[0]
    capacity = tok_rows // 4
    buffer_rows = experts * capacity
    highest = lax.Precision.HIGHEST
    matches = (routing[:, :, None] == jnp.arange(experts, dtype=jnp.int32)[None, None, :]).astype(
        jnp.int32
    )
    per_token = jnp.sum(matches, axis=1)
    earlier = jnp.cumsum(per_token, axis=0) - per_token
    destination = routing * capacity + jnp.take_along_axis(earlier, routing, axis=1)
    placed = (
        destination[:, :, None] == jnp.arange(buffer_rows, dtype=jnp.int32)[None, None, :]
    ).astype(jnp.float32)
    membership = jnp.sum(placed, axis=1)
    weighting = jnp.sum(placed * gates[:, :, None], axis=1)
    quarter = tokens.shape[1]
    rows = jnp.einsum(
        "tr,td->rd",
        membership.astype(jnp.bfloat16),
        tokens,
        preferred_element_type=jnp.float32,
    ).astype(jnp.bfloat16)
    scaled = jnp.einsum(
        "tr,td->rd", weighting, cotangent.astype(jnp.float32), precision=highest
    ).astype(jnp.bfloat16)
    step = capacity // CHUNKS
    send = jnp.concatenate(
        [
            rows.reshape(devices, local_experts, CHUNKS, step, quarter),
            scaled.reshape(devices, local_experts, CHUNKS, step, quarter),
        ],
        axis=3,
    )
    spread = dispatch(send.reshape(devices, -1, quarter), groups, 0)
    whole = spread.reshape(devices, local_experts, CHUNKS, 2 * step, groups * quarter)
    back_out, back_grad, d_w_in, d_w_out = [], [], None, None
    for c in range(CHUNKS):
        with jax.named_scope(f"slot_chunk{c}"):
            b_out, b_grad, g_in, g_out = expert_chunk(
                whole[:, :, c, :step], whole[:, :, c, step:], w_in, w_out, quarter, 1 + c
            )
        back_out.append(b_out)
        back_grad.append(b_grad)
        d_w_in = g_in if d_w_in is None else d_w_in + g_in
        d_w_out = g_out if d_w_out is None else d_w_out + g_out
    back_out = jnp.concatenate(back_out, axis=2).reshape(buffer_rows, quarter).astype(jnp.float32)
    back_grad = jnp.concatenate(back_grad, axis=2).reshape(buffer_rows, quarter).astype(jnp.float32)
    mixed = jnp.einsum("tr,rd->td", weighting, back_out, precision=highest).astype(jnp.bfloat16)
    d_tokens = jnp.einsum("tr,rd->td", membership, back_grad, precision=highest).astype(
        jnp.bfloat16
    )
    return (mixed, d_tokens, d_w_in.astype(jnp.bfloat16), d_w_out.astype(jnp.bfloat16))


def solution(mesh):
    placed = (
        P("expert", "tensor"),
        P("expert", "tensor"),
        P("expert", None),
        P("expert", None),
        P("expert", None, "tensor"),
        P("expert", "tensor", None),
    )
    return jax.shard_map(
        shards,
        mesh=mesh,
        in_specs=placed,
        out_specs=(
            P("expert", "tensor"),
            P("expert", "tensor"),
            P("expert", None, "tensor"),
            P("expert", "tensor", None),
        ),
        check_vma=False,
    )
```

```python
import jax
import jax.numpy as jnp
from jax import lax
from jax.experimental import pallas as pl
from jax.experimental.pallas import tpu as pltpu
from jax.sharding import PartitionSpec as P

CHUNKS = 2


def _a2a_kernel(x_ref, o_ref, send_sem, recv_sem, local_sem):
    n = x_ref.shape[0]
    me = lax.axis_index("expert")
    tau = lax.axis_index("tensor")
    barrier = pltpu.get_barrier_semaphore()

    def greet(k, carry):
        peer = lax.rem(me + k, n)
        pl.semaphore_signal(
            barrier, inc=1, device_id=(peer, tau), device_id_type=pl.DeviceIdType.MESH
        )
        return carry

    lax.fori_loop(1, n, greet, 0)
    pl.semaphore_wait(barrier, n - 1)

    local = pltpu.make_async_copy(x_ref.at[me], o_ref.at[me], local_sem)
    local.start()

    def push(k, carry):
        peer = lax.rem(me + k, n)
        pltpu.make_async_remote_copy(
            src_ref=x_ref.at[peer],
            dst_ref=o_ref.at[me],
            send_sem=send_sem.at[k],
            recv_sem=recv_sem.at[k],
            device_id=(peer, tau),
            device_id_type=pl.DeviceIdType.MESH,
        ).start()
        return carry

    lax.fori_loop(1, n, push, 0)

    def settle(k, carry):
        peer = lax.rem(me + k, n)
        source = lax.rem(me + n - k, n)
        pltpu.make_async_remote_copy(
            src_ref=x_ref.at[peer],
            dst_ref=o_ref.at[source],
            send_sem=send_sem.at[k],
            recv_sem=recv_sem.at[k],
            device_id=(peer, tau),
            device_id_type=pl.DeviceIdType.MESH,
        ).wait()
        return carry

    lax.fori_loop(1, n, settle, 0)
    local.wait()


def expert_all_to_all(x, collective_id):
    n = x.shape[0]
    return pl.pallas_call(
        _a2a_kernel,
        out_shape=jax.ShapeDtypeStruct(x.shape, x.dtype),
        in_specs=[pl.BlockSpec(memory_space=pl.ANY)],
        out_specs=pl.BlockSpec(memory_space=pl.ANY),
        scratch_shapes=[
            pltpu.SemaphoreType.DMA((n,)),
            pltpu.SemaphoreType.DMA((n,)),
            pltpu.SemaphoreType.DMA(()),
        ],
        compiler_params=pltpu.CompilerParams(collective_id=collective_id, has_side_effects=True),
        cost_estimate=pl.CostEstimate(
            flops=0, transcendentals=0, bytes_accessed=2 * x.size * x.dtype.itemsize
        ),
    )(x)


def _dispatch_kernel(x_ref, o_ref, xz_send, xz_recv, y_send, y_recv, local_sem):
    n, width = x_ref.shape[0], x_ref.shape[-1]
    groups = o_ref.shape[-1] // width
    me = lax.axis_index("expert")
    tau = lax.axis_index("tensor")
    barrier = pltpu.get_barrier_semaphore()

    def cols(g):
        return pl.ds(pl.multiple_of(g * width, 128), width)

    def greet(k, carry):
        pl.semaphore_signal(
            barrier, inc=1, device_id=(lax.rem(me + k, n), tau), device_id_type=pl.DeviceIdType.MESH
        )
        return carry

    lax.fori_loop(1, n, greet, 0)
    for j in range(1, groups):
        pl.semaphore_signal(
            barrier, inc=1, device_id=(me, lax.rem(tau + j, groups)), device_id_type=pl.DeviceIdType.MESH
        )
    pl.semaphore_wait(barrier, n - 1 + groups - 1)

    local = pltpu.make_async_copy(x_ref.at[me], o_ref.at[:, :, me, :, cols(tau)], local_sem)
    local.start()

    def xz_copy(k):
        peer = lax.rem(me + k, n)
        return pltpu.make_async_remote_copy(
            src_ref=x_ref.at[peer],
            dst_ref=o_ref.at[:, :, me, :, cols(tau)],
            send_sem=xz_send.at[k],
            recv_sem=xz_recv.at[k],
            device_id=(peer, tau),
            device_id_type=pl.DeviceIdType.MESH,
        )

    def xz_arrival(k):
        peer = lax.rem(me + k, n)
        source = lax.rem(me + n - k, n)
        return pltpu.make_async_remote_copy(
            src_ref=x_ref.at[peer],
            dst_ref=o_ref.at[:, :, source, :, cols(tau)],
            send_sem=xz_send.at[k],
            recv_sem=xz_recv.at[k],
            device_id=(peer, tau),
            device_id_type=pl.DeviceIdType.MESH,
        )

    def y_copy(j, k):
        source = lax.rem(me + n - k, n)
        return pltpu.make_async_remote_copy(
            src_ref=o_ref.at[:, :, source, :, cols(tau)],
            dst_ref=o_ref.at[:, :, source, :, cols(tau)],
            send_sem=y_send.at[j - 1, k],
            recv_sem=y_recv.at[j - 1, k],
            device_id=(me, lax.rem(tau + j, groups)),
            device_id_type=pl.DeviceIdType.MESH,
        )

    def y_arrival(j, k):
        source = lax.rem(me + n - k, n)
        return pltpu.make_async_remote_copy(
            src_ref=o_ref.at[:, :, source, :, cols(tau)],
            dst_ref=o_ref.at[:, :, source, :, cols(lax.rem(tau + groups - j, groups))],
            send_sem=y_send.at[j - 1, k],
            recv_sem=y_recv.at[j - 1, k],
            device_id=(me, lax.rem(tau + j, groups)),
            device_id_type=pl.DeviceIdType.MESH,
        )

    def push(k, carry):
        xz_copy(k).start()
        return carry

    lax.fori_loop(1, n, push, 0)

    local.wait()
    for j in range(1, groups):
        y_copy(j, 0).start()

    def forward(k, carry):
        xz_arrival(k).wait_recv()
        for j in range(1, groups):
            y_copy(j, k).start()
        return carry

    lax.fori_loop(1, n, forward, 0)

    def settle(k, carry):
        xz_copy(k).wait_send()
        return carry

    lax.fori_loop(1, n, settle, 0)

    def settle_y(k, carry):
        for j in range(1, groups):
            y_copy(j, k).wait_send()
            y_arrival(j, k).wait_recv()
        return carry

    lax.fori_loop(0, n, settle_y, 0)


def dispatch(x, groups, collective_id):
    n, chunks, kinds, slots, width = x.shape
    return pl.pallas_call(
        _dispatch_kernel,
        out_shape=jax.ShapeDtypeStruct((chunks, kinds, n, slots, groups * width), x.dtype),
        in_specs=[pl.BlockSpec(memory_space=pl.ANY)],
        out_specs=pl.BlockSpec(memory_space=pl.ANY),
        scratch_shapes=[
            pltpu.SemaphoreType.DMA((n,)),
            pltpu.SemaphoreType.DMA((n,)),
            pltpu.SemaphoreType.DMA((groups - 1, n)),
            pltpu.SemaphoreType.DMA((groups - 1, n)),
            pltpu.SemaphoreType.DMA(()),
        ],
        compiler_params=pltpu.CompilerParams(collective_id=collective_id, has_side_effects=True),
        cost_estimate=pl.CostEstimate(
            flops=0, transcendentals=0, bytes_accessed=(1 + 2 * groups) * x.size * x.dtype.itemsize
        ),
    )(x)


def expert_chunk(expert_rows, expert_scaled, w_in, w_out, quarter, collective_id):
    slots = expert_rows.shape[2]
    preact = jnp.einsum("nesd,edh->nesh", expert_rows, w_in, preferred_element_type=jnp.float32)
    sigmoid_val = jax.nn.sigmoid(preact)
    hidden = (preact * sigmoid_val).astype(jnp.bfloat16)
    out_part = jnp.einsum("nesh,ehd->nesd", hidden, w_out, preferred_element_type=jnp.float32)
    grad_hidden = jnp.einsum(
        "nesd,ehd->nesh", expert_scaled, w_out, preferred_element_type=jnp.float32
    )
    grad_preact = (grad_hidden * sigmoid_val * (1.0 + preact * (1.0 - sigmoid_val))).astype(
        jnp.bfloat16
    )
    d_w_out = jnp.einsum(
        "nesh,nesd->ehd", hidden, expert_scaled, preferred_element_type=jnp.float32
    )
    d_w_in = jnp.einsum(
        "nesd,nesh->edh", expert_rows, grad_preact, preferred_element_type=jnp.float32
    )
    grad_part = jnp.einsum("nesh,edh->nesd", grad_preact, w_in, preferred_element_type=jnp.float32)
    parts = jnp.concatenate(
        [out_part.astype(jnp.bfloat16), grad_part.astype(jnp.bfloat16)], axis=2
    )
    sums = lax.psum_scatter(parts, "tensor", scatter_dimension=3, tiled=True)
    back = expert_all_to_all(sums.reshape(sums.shape[0], -1, quarter), collective_id).reshape(sums.shape)
    return back[:, :, :slots], back[:, :, slots:], d_w_in, d_w_out


def shards(tokens, cotangent, routing, gates, w_in, w_out):
    devices = lax.axis_size("expert")
    groups = lax.axis_size("tensor")
    local_experts = w_in.shape[0]
    experts = devices * local_experts
    tok_rows = routing.shape[0]
    capacity = tok_rows // 4
    buffer_rows = experts * capacity
    highest = lax.Precision.HIGHEST
    matches = (routing[:, :, None] == jnp.arange(experts, dtype=jnp.int32)[None, None, :]).astype(
        jnp.int32
    )
    per_token = jnp.sum(matches, axis=1)
    earlier = jnp.cumsum(per_token, axis=0) - per_token
    destination = routing * capacity + jnp.take_along_axis(earlier, routing, axis=1)
    placed = (
        destination[:, :, None] == jnp.arange(buffer_rows, dtype=jnp.int32)[None, None, :]
    ).astype(jnp.float32)
    membership = jnp.sum(placed, axis=1)
    weighting = jnp.sum(placed * gates[:, :, None], axis=1)
    quarter = tokens.shape[1]
    rows = jnp.einsum(
        "tr,td->rd",
        membership.astype(jnp.bfloat16),
        tokens,
        preferred_element_type=jnp.float32,
    ).astype(jnp.bfloat16)
    scaled = jnp.einsum(
        "tr,td->rd", weighting, cotangent.astype(jnp.float32), precision=highest
    ).astype(jnp.bfloat16)
    step = capacity // CHUNKS
    send = jnp.stack(
        [
            rows.reshape(devices, local_experts * CHUNKS, step, quarter),
            scaled.reshape(devices, local_experts * CHUNKS, step, quarter),
        ],
        axis=2,
    )
    whole = dispatch(send, groups, 0)
    back_out, back_grad, d_w_in, d_w_out = [], [], None, None
    for c in range(CHUNKS):
        with jax.named_scope(f"slot_chunk{c}"):
            b_out, b_grad, g_in, g_out = expert_chunk(
                whole[c, 0][:, None], whole[c, 1][:, None], w_in, w_out, quarter, 1 + c
            )
        back_out.append(b_out)
        back_grad.append(b_grad)
        d_w_in = g_in if d_w_in is None else d_w_in + g_in
        d_w_out = g_out if d_w_out is None else d_w_out + g_out
    back_out = jnp.concatenate(back_out, axis=2).reshape(buffer_rows, quarter).astype(jnp.float32)
    back_grad = jnp.concatenate(back_grad, axis=2).reshape(buffer_rows, quarter).astype(jnp.float32)
    mixed = jnp.einsum("tr,rd->td", weighting, back_out, precision=highest).astype(jnp.bfloat16)
    d_tokens = jnp.einsum("tr,rd->td", membership, back_grad, precision=highest).astype(
        jnp.bfloat16
    )
    return (mixed, d_tokens, d_w_in.astype(jnp.bfloat16), d_w_out.astype(jnp.bfloat16))


def solution(mesh):
    placed = (
        P("expert", "tensor"),
        P("expert", "tensor"),
        P("expert", None),
        P("expert", None),
        P("expert", None, "tensor"),
        P("expert", "tensor", None),
    )
    return jax.shard_map(
        shards,
        mesh=mesh,
        in_specs=placed,
        out_specs=(
            P("expert", "tensor"),
            P("expert", "tensor"),
            P("expert", None, "tensor"),
            P("expert", "tensor", None),
        ),
        check_vma=False,
    )
```

```python
import jax
import jax.numpy as jnp
from jax import lax
from jax.experimental import pallas as pl
from jax.experimental.pallas import tpu as pltpu
from jax.sharding import PartitionSpec as P

CHUNKS = 2


def _a2a_kernel(x_ref, o_ref, send_sem, recv_sem, local_sem):
    n = x_ref.shape[0]
    me = lax.axis_index("expert")
    tau = lax.axis_index("tensor")
    barrier = pltpu.get_barrier_semaphore()

    def greet(k, carry):
        peer = lax.rem(me + k, n)
        pl.semaphore_signal(
            barrier, inc=1, device_id=(peer, tau), device_id_type=pl.DeviceIdType.MESH
        )
        return carry

    lax.fori_loop(1, n, greet, 0)
    pl.semaphore_wait(barrier, n - 1)

    local = pltpu.make_async_copy(x_ref.at[me], o_ref.at[me], local_sem)
    local.start()

    def push(k, carry):
        peer = lax.rem(me + k, n)
        pltpu.make_async_remote_copy(
            src_ref=x_ref.at[peer],
            dst_ref=o_ref.at[me],
            send_sem=send_sem.at[k],
            recv_sem=recv_sem.at[k],
            device_id=(peer, tau),
            device_id_type=pl.DeviceIdType.MESH,
        ).start()
        return carry

    lax.fori_loop(1, n, push, 0)

    def settle(k, carry):
        peer = lax.rem(me + k, n)
        source = lax.rem(me + n - k, n)
        pltpu.make_async_remote_copy(
            src_ref=x_ref.at[peer],
            dst_ref=o_ref.at[source],
            send_sem=send_sem.at[k],
            recv_sem=recv_sem.at[k],
            device_id=(peer, tau),
            device_id_type=pl.DeviceIdType.MESH,
        ).wait()
        return carry

    lax.fori_loop(1, n, settle, 0)
    local.wait()


def expert_all_to_all(x, collective_id):
    n = x.shape[0]
    return pl.pallas_call(
        _a2a_kernel,
        out_shape=jax.ShapeDtypeStruct(x.shape, x.dtype),
        in_specs=[pl.BlockSpec(memory_space=pltpu.VMEM)],
        out_specs=pl.BlockSpec(memory_space=pltpu.VMEM),
        scratch_shapes=[
            pltpu.SemaphoreType.DMA((n,)),
            pltpu.SemaphoreType.DMA((n,)),
            pltpu.SemaphoreType.DMA(()),
        ],
        compiler_params=pltpu.CompilerParams(collective_id=collective_id, has_side_effects=True),
        cost_estimate=pl.CostEstimate(
            flops=0, transcendentals=0, bytes_accessed=2 * x.size * x.dtype.itemsize
        ),
    )(x)


def expert_chunk(rows, scaled, w_in, w_out, quarter, ids):
    slots = rows.shape[2]
    send = jnp.concatenate([rows, scaled], axis=2)
    arrived = expert_all_to_all(send.reshape(send.shape[0], -1, quarter), ids[0]).reshape(send.shape)
    whole = lax.all_gather(arrived, "tensor", axis=3, tiled=True)
    expert_rows = whole[:, :, :slots]
    expert_scaled = whole[:, :, slots:]
    preact = jnp.einsum("nesd,edh->nesh", expert_rows, w_in, preferred_element_type=jnp.float32)
    sigmoid_val = jax.nn.sigmoid(preact)
    hidden = (preact * sigmoid_val).astype(jnp.bfloat16)
    out_part = jnp.einsum("nesh,ehd->nesd", hidden, w_out, preferred_element_type=jnp.float32)
    grad_hidden = jnp.einsum(
        "nesd,ehd->nesh", expert_scaled, w_out, preferred_element_type=jnp.float32
    )
    grad_preact = (grad_hidden * sigmoid_val * (1.0 + preact * (1.0 - sigmoid_val))).astype(
        jnp.bfloat16
    )
    d_w_out = jnp.einsum(
        "nesh,nesd->ehd", hidden, expert_scaled, preferred_element_type=jnp.float32
    )
    d_w_in = jnp.einsum(
        "nesd,nesh->edh", expert_rows, grad_preact, preferred_element_type=jnp.float32
    )
    grad_part = jnp.einsum("nesh,edh->nesd", grad_preact, w_in, preferred_element_type=jnp.float32)
    parts = jnp.concatenate(
        [out_part.astype(jnp.bfloat16), grad_part.astype(jnp.bfloat16)], axis=2
    )
    sums = lax.psum_scatter(parts, "tensor", scatter_dimension=3, tiled=True)
    back = expert_all_to_all(sums.reshape(sums.shape[0], -1, quarter), ids[1]).reshape(sums.shape)
    return back[:, :, :slots], back[:, :, slots:], d_w_in, d_w_out


def shards(tokens, cotangent, routing, gates, w_in, w_out):
    devices = lax.axis_size("expert")
    local_experts = w_in.shape[0]
    experts = devices * local_experts
    tok_rows = routing.shape[0]
    capacity = tok_rows // 4
    buffer_rows = experts * capacity
    highest = lax.Precision.HIGHEST
    matches = (routing[:, :, None] == jnp.arange(experts, dtype=jnp.int32)[None, None, :]).astype(
        jnp.int32
    )
    per_token = jnp.sum(matches, axis=1)
    earlier = jnp.cumsum(per_token, axis=0) - per_token
    destination = routing * capacity + jnp.take_along_axis(earlier, routing, axis=1)
    placed = (
        destination[:, :, None] == jnp.arange(buffer_rows, dtype=jnp.int32)[None, None, :]
    ).astype(jnp.float32)
    membership = jnp.sum(placed, axis=1)
    weighting = jnp.sum(placed * gates[:, :, None], axis=1)
    quarter = tokens.shape[1]
    rows = jnp.einsum(
        "tr,td->rd",
        membership.astype(jnp.bfloat16),
        tokens,
        preferred_element_type=jnp.float32,
    ).astype(jnp.bfloat16)
    scaled = jnp.einsum(
        "tr,td->rd", weighting, cotangent.astype(jnp.float32), precision=highest
    ).astype(jnp.bfloat16)
    rows = rows.reshape(devices, local_experts, capacity, quarter)
    scaled = scaled.reshape(devices, local_experts, capacity, quarter)
    step = capacity // CHUNKS
    back_out, back_grad, d_w_in, d_w_out = [], [], None, None
    for c in range(CHUNKS):
        window = slice(c * step, (c + 1) * step)
        with jax.named_scope(f"slot_chunk{c}"):
            b_out, b_grad, g_in, g_out = expert_chunk(
                rows[:, :, window], scaled[:, :, window], w_in, w_out, quarter, (2 * c, 2 * c + 1)
            )
        back_out.append(b_out)
        back_grad.append(b_grad)
        d_w_in = g_in if d_w_in is None else d_w_in + g_in
        d_w_out = g_out if d_w_out is None else d_w_out + g_out
    back_out = jnp.concatenate(back_out, axis=2).reshape(buffer_rows, quarter).astype(jnp.float32)
    back_grad = jnp.concatenate(back_grad, axis=2).reshape(buffer_rows, quarter).astype(jnp.float32)
    mixed = jnp.einsum("tr,rd->td", weighting, back_out, precision=highest).astype(jnp.bfloat16)
    d_tokens = jnp.einsum("tr,rd->td", membership, back_grad, precision=highest).astype(
        jnp.bfloat16
    )
    return (mixed, d_tokens, d_w_in.astype(jnp.bfloat16), d_w_out.astype(jnp.bfloat16))


def solution(mesh):
    placed = (
        P("expert", "tensor"),
        P("expert", "tensor"),
        P("expert", None),
        P("expert", None),
        P("expert", None, "tensor"),
        P("expert", "tensor", None),
    )
    return jax.shard_map(
        shards,
        mesh=mesh,
        in_specs=placed,
        out_specs=(
            P("expert", "tensor"),
            P("expert", "tensor"),
            P("expert", None, "tensor"),
            P("expert", "tensor", None),
        ),
        check_vma=False,
    )
```

```python
import jax
import jax.numpy as jnp
from jax import lax
from jax.experimental import pallas as pl
from jax.experimental.pallas import tpu as pltpu
from jax.sharding import PartitionSpec as P

CHUNKS = 2


def _a2a_kernel(x_ref, o_ref, send_sem, recv_sem, local_sem):
    n = x_ref.shape[0]
    me = lax.axis_index("expert")
    tau = lax.axis_index("tensor")
    barrier = pltpu.get_barrier_semaphore()

    def greet(k, carry):
        peer = lax.rem(me + k, n)
        pl.semaphore_signal(
            barrier, inc=1, device_id=(peer, tau), device_id_type=pl.DeviceIdType.MESH
        )
        return carry

    lax.fori_loop(1, n, greet, 0)
    pl.semaphore_wait(barrier, n - 1)

    local = pltpu.make_async_copy(x_ref.at[me], o_ref.at[me], local_sem)
    local.start()

    def push(k, carry):
        peer = lax.rem(me + k, n)
        pltpu.make_async_remote_copy(
            src_ref=x_ref.at[peer],
            dst_ref=o_ref.at[me],
            send_sem=send_sem.at[k],
            recv_sem=recv_sem.at[k],
            device_id=(peer, tau),
            device_id_type=pl.DeviceIdType.MESH,
        ).start()
        return carry

    lax.fori_loop(1, n, push, 0)

    def settle(k, carry):
        peer = lax.rem(me + k, n)
        source = lax.rem(me + n - k, n)
        pltpu.make_async_remote_copy(
            src_ref=x_ref.at[peer],
            dst_ref=o_ref.at[source],
            send_sem=send_sem.at[k],
            recv_sem=recv_sem.at[k],
            device_id=(peer, tau),
            device_id_type=pl.DeviceIdType.MESH,
        ).wait()
        return carry

    lax.fori_loop(1, n, settle, 0)
    local.wait()


def expert_all_to_all(x, collective_id):
    n = x.shape[0]
    return pl.pallas_call(
        _a2a_kernel,
        out_shape=jax.ShapeDtypeStruct(x.shape, x.dtype),
        in_specs=[pl.BlockSpec(memory_space=pl.ANY)],
        out_specs=pl.BlockSpec(memory_space=pl.ANY),
        scratch_shapes=[
            pltpu.SemaphoreType.DMA((n,)),
            pltpu.SemaphoreType.DMA((n,)),
            pltpu.SemaphoreType.DMA(()),
        ],
        compiler_params=pltpu.CompilerParams(collective_id=collective_id, has_side_effects=True),
        cost_estimate=pl.CostEstimate(
            flops=0, transcendentals=0, bytes_accessed=2 * x.size * x.dtype.itemsize
        ),
    )(x)


def expert_chunk(rows, scaled, w_in, w_out, quarter, ids):
    slots = rows.shape[2]
    send = jnp.concatenate([rows, scaled], axis=2)
    arrived = expert_all_to_all(send.reshape(send.shape[0], -1, quarter), ids[0]).reshape(send.shape)
    whole = lax.all_gather(arrived, "tensor", axis=3, tiled=True)
    expert_rows = whole[:, :, :slots]
    expert_scaled = whole[:, :, slots:]
    preact = jnp.einsum("nesd,edh->nesh", expert_rows, w_in, preferred_element_type=jnp.float32)
    sigmoid_val = jax.nn.sigmoid(preact)
    hidden = (preact * sigmoid_val).astype(jnp.bfloat16)
    out_part = jnp.einsum("nesh,ehd->nesd", hidden, w_out, preferred_element_type=jnp.float32)
    grad_hidden = jnp.einsum(
        "nesd,ehd->nesh", expert_scaled, w_out, preferred_element_type=jnp.float32
    )
    grad_preact = (grad_hidden * sigmoid_val * (1.0 + preact * (1.0 - sigmoid_val))).astype(
        jnp.bfloat16
    )
    d_w_out = jnp.einsum(
        "nesh,nesd->ehd", hidden, expert_scaled, preferred_element_type=jnp.float32
    )
    d_w_in = jnp.einsum(
        "nesd,nesh->edh", expert_rows, grad_preact, preferred_element_type=jnp.float32
    )
    grad_part = jnp.einsum("nesh,edh->nesd", grad_preact, w_in, preferred_element_type=jnp.float32)
    parts = jnp.concatenate(
        [out_part.astype(jnp.bfloat16), grad_part.astype(jnp.bfloat16)], axis=2
    )
    sums = lax.psum_scatter(parts, "tensor", scatter_dimension=3, tiled=True)
    back = expert_all_to_all(sums.reshape(sums.shape[0], -1, quarter), ids[1]).reshape(sums.shape)
    return back[:, :, :slots], back[:, :, slots:], d_w_in, d_w_out


def shards(tokens, cotangent, routing, gates, w_in, w_out):
    devices = lax.axis_size("expert")
    local_experts = w_in.shape[0]
    experts = devices * local_experts
    tok_rows = routing.shape[0]
    capacity = tok_rows // 4
    buffer_rows = experts * capacity
    highest = lax.Precision.HIGHEST
    matches = (routing[:, :, None] == jnp.arange(experts, dtype=jnp.int32)[None, None, :]).astype(
        jnp.int32
    )
    per_token = jnp.sum(matches, axis=1)
    earlier = jnp.cumsum(per_token, axis=0) - per_token
    destination = routing * capacity + jnp.sum(matches * earlier[:, None, :], axis=2)
    placed = (
        destination[:, :, None] == jnp.arange(buffer_rows, dtype=jnp.int32)[None, None, :]
    ).astype(jnp.float32)
    membership = jnp.sum(placed, axis=1)
    weighting = jnp.sum(placed * gates[:, :, None], axis=1)
    quarter = tokens.shape[1]
    rows = jnp.einsum(
        "tr,td->rd",
        membership.astype(jnp.bfloat16),
        tokens,
        preferred_element_type=jnp.float32,
    ).astype(jnp.bfloat16)
    scaled = jnp.einsum(
        "tr,td->rd", weighting, cotangent.astype(jnp.float32), precision=highest
    ).astype(jnp.bfloat16)
    rows = rows.reshape(devices, local_experts, capacity, quarter)
    scaled = scaled.reshape(devices, local_experts, capacity, quarter)
    step = capacity // CHUNKS
    back_out, back_grad, d_w_in, d_w_out = [], [], None, None
    for c in range(CHUNKS):
        window = slice(c * step, (c + 1) * step)
        with jax.named_scope(f"slot_chunk{c}"):
            b_out, b_grad, g_in, g_out = expert_chunk(
                rows[:, :, window], scaled[:, :, window], w_in, w_out, quarter, (2 * c, 2 * c + 1)
            )
        back_out.append(b_out)
        back_grad.append(b_grad)
        d_w_in = g_in if d_w_in is None else d_w_in + g_in
        d_w_out = g_out if d_w_out is None else d_w_out + g_out
    back_out = jnp.concatenate(back_out, axis=2).reshape(buffer_rows, quarter)
    back_grad = jnp.concatenate(back_grad, axis=2).reshape(buffer_rows, quarter)
    gate_hi = weighting.astype(jnp.bfloat16)
    rest = weighting - gate_hi.astype(jnp.float32)
    gate_mid = rest.astype(jnp.bfloat16)
    gate_lo = (rest - gate_mid.astype(jnp.float32)).astype(jnp.bfloat16)
    mixed = sum(
        jnp.einsum("tr,rd->td", part, back_out, preferred_element_type=jnp.float32)
        for part in (gate_lo, gate_mid, gate_hi)
    ).astype(jnp.bfloat16)
    d_tokens = jnp.einsum(
        "tr,rd->td", membership.astype(jnp.bfloat16), back_grad, preferred_element_type=jnp.float32
    ).astype(jnp.bfloat16)
    return (mixed, d_tokens, d_w_in.astype(jnp.bfloat16), d_w_out.astype(jnp.bfloat16))


def solution(mesh):
    placed = (
        P("expert", "tensor"),
        P("expert", "tensor"),
        P("expert", None),
        P("expert", None),
        P("expert", None, "tensor"),
        P("expert", "tensor", None),
    )
    return jax.shard_map(
        shards,
        mesh=mesh,
        in_specs=placed,
        out_specs=(
            P("expert", "tensor"),
            P("expert", "tensor"),
            P("expert", None, "tensor"),
            P("expert", "tensor", None),
        ),
        check_vma=False,
    )
```

```python
import jax
import jax.numpy as jnp
from jax import lax
from jax.experimental import pallas as pl
from jax.experimental.pallas import tpu as pltpu
from jax.sharding import PartitionSpec as P

CHUNKS = 2


def _a2a_kernel(x_ref, o_ref, send_sem, recv_sem, local_sem):
    n = x_ref.shape[0]
    me = lax.axis_index("expert")
    tau = lax.axis_index("tensor")
    barrier = pltpu.get_barrier_semaphore()

    def greet(k, carry):
        peer = lax.rem(me + k, n)
        pl.semaphore_signal(
            barrier, inc=1, device_id=(peer, tau), device_id_type=pl.DeviceIdType.MESH
        )
        return carry

    lax.fori_loop(1, n, greet, 0)
    pl.semaphore_wait(barrier, n - 1)

    local = pltpu.make_async_copy(x_ref.at[me], o_ref.at[me], local_sem)
    local.start()

    def push(i, carry):
        half = i // 2 + 1
        k = half + (i % 2) * (n - 2 * half)
        peer = lax.rem(me + k, n)
        pltpu.make_async_remote_copy(
            src_ref=x_ref.at[peer],
            dst_ref=o_ref.at[me],
            send_sem=send_sem.at[k],
            recv_sem=recv_sem.at[k],
            device_id=(peer, tau),
            device_id_type=pl.DeviceIdType.MESH,
        ).start()
        return carry

    lax.fori_loop(0, n - 1, push, 0)

    def settle(k, carry):
        peer = lax.rem(me + k, n)
        source = lax.rem(me + n - k, n)
        pltpu.make_async_remote_copy(
            src_ref=x_ref.at[peer],
            dst_ref=o_ref.at[source],
            send_sem=send_sem.at[k],
            recv_sem=recv_sem.at[k],
            device_id=(peer, tau),
            device_id_type=pl.DeviceIdType.MESH,
        ).wait()
        return carry

    lax.fori_loop(1, n, settle, 0)
    local.wait()


def expert_all_to_all(x, collective_id):
    n = x.shape[0]
    return pl.pallas_call(
        _a2a_kernel,
        out_shape=jax.ShapeDtypeStruct(x.shape, x.dtype),
        in_specs=[pl.BlockSpec(memory_space=pl.ANY)],
        out_specs=pl.BlockSpec(memory_space=pl.ANY),
        scratch_shapes=[
            pltpu.SemaphoreType.DMA((n,)),
            pltpu.SemaphoreType.DMA((n,)),
            pltpu.SemaphoreType.DMA(()),
        ],
        compiler_params=pltpu.CompilerParams(collective_id=collective_id, has_side_effects=True),
        cost_estimate=pl.CostEstimate(
            flops=0, transcendentals=0, bytes_accessed=2 * x.size * x.dtype.itemsize
        ),
    )(x)


def expert_chunk(rows, scaled, w_in, w_out, quarter, ids):
    slots = rows.shape[2]
    send = jnp.concatenate([rows, scaled], axis=2)
    arrived = expert_all_to_all(send.reshape(send.shape[0], -1, quarter), ids[0]).reshape(send.shape)
    whole = lax.all_gather(arrived, "tensor", axis=3, tiled=True)
    expert_rows = whole[:, :, :slots]
    expert_scaled = whole[:, :, slots:]
    preact = jnp.einsum("nesd,edh->nesh", expert_rows, w_in, preferred_element_type=jnp.float32)
    sigmoid_val = jax.nn.sigmoid(preact)
    hidden = (preact * sigmoid_val).astype(jnp.bfloat16)
    out_part = jnp.einsum("nesh,ehd->nesd", hidden, w_out, preferred_element_type=jnp.float32)
    grad_hidden = jnp.einsum(
        "nesd,ehd->nesh", expert_scaled, w_out, preferred_element_type=jnp.float32
    )
    grad_preact = (grad_hidden * sigmoid_val * (1.0 + preact * (1.0 - sigmoid_val))).astype(
        jnp.bfloat16
    )
    d_w_out = jnp.einsum(
        "nesh,nesd->ehd", hidden, expert_scaled, preferred_element_type=jnp.float32
    )
    d_w_in = jnp.einsum(
        "nesd,nesh->edh", expert_rows, grad_preact, preferred_element_type=jnp.float32
    )
    grad_part = jnp.einsum("nesh,edh->nesd", grad_preact, w_in, preferred_element_type=jnp.float32)
    parts = jnp.concatenate(
        [out_part.astype(jnp.bfloat16), grad_part.astype(jnp.bfloat16)], axis=2
    )
    sums = lax.psum_scatter(parts, "tensor", scatter_dimension=3, tiled=True)
    back = expert_all_to_all(sums.reshape(sums.shape[0], -1, quarter), ids[1]).reshape(sums.shape)
    return back[:, :, :slots], back[:, :, slots:], d_w_in, d_w_out


def shards(tokens, cotangent, routing, gates, w_in, w_out):
    devices = lax.axis_size("expert")
    local_experts = w_in.shape[0]
    experts = devices * local_experts
    tok_rows = routing.shape[0]
    capacity = tok_rows // 4
    buffer_rows = experts * capacity
    highest = lax.Precision.HIGHEST
    matches = (routing[:, :, None] == jnp.arange(experts, dtype=jnp.int32)[None, None, :]).astype(
        jnp.int32
    )
    per_token = jnp.sum(matches, axis=1)
    earlier = jnp.cumsum(per_token, axis=0) - per_token
    destination = routing * capacity + jnp.take_along_axis(earlier, routing, axis=1)
    placed = (
        destination[:, :, None] == jnp.arange(buffer_rows, dtype=jnp.int32)[None, None, :]
    ).astype(jnp.float32)
    membership = jnp.sum(placed, axis=1)
    weighting = jnp.sum(placed * gates[:, :, None], axis=1)
    quarter = tokens.shape[1]
    rows = jnp.einsum(
        "tr,td->rd",
        membership.astype(jnp.bfloat16),
        tokens,
        preferred_element_type=jnp.float32,
    ).astype(jnp.bfloat16)
    scaled = jnp.einsum(
        "tr,td->rd", weighting, cotangent.astype(jnp.float32), precision=highest
    ).astype(jnp.bfloat16)
    rows = rows.reshape(devices, local_experts, capacity, quarter)
    scaled = scaled.reshape(devices, local_experts, capacity, quarter)
    step = capacity // CHUNKS
    back_out, back_grad, d_w_in, d_w_out = [], [], None, None
    for c in range(CHUNKS):
        window = slice(c * step, (c + 1) * step)
        with jax.named_scope(f"slot_chunk{c}"):
            b_out, b_grad, g_in, g_out = expert_chunk(
                rows[:, :, window], scaled[:, :, window], w_in, w_out, quarter, (2 * c, 2 * c + 1)
            )
        back_out.append(b_out)
        back_grad.append(b_grad)
        d_w_in = g_in if d_w_in is None else d_w_in + g_in
        d_w_out = g_out if d_w_out is None else d_w_out + g_out
    back_out = jnp.concatenate(back_out, axis=2).reshape(buffer_rows, quarter).astype(jnp.float32)
    back_grad = jnp.concatenate(back_grad, axis=2).reshape(buffer_rows, quarter).astype(jnp.float32)
    mixed = jnp.einsum("tr,rd->td", weighting, back_out, precision=highest).astype(jnp.bfloat16)
    d_tokens = jnp.einsum("tr,rd->td", membership, back_grad, precision=highest).astype(
        jnp.bfloat16
    )
    return (mixed, d_tokens, d_w_in.astype(jnp.bfloat16), d_w_out.astype(jnp.bfloat16))


def solution(mesh):
    placed = (
        P("expert", "tensor"),
        P("expert", "tensor"),
        P("expert", None),
        P("expert", None),
        P("expert", None, "tensor"),
        P("expert", "tensor", None),
    )
    return jax.shard_map(
        shards,
        mesh=mesh,
        in_specs=placed,
        out_specs=(
            P("expert", "tensor"),
            P("expert", "tensor"),
            P("expert", None, "tensor"),
            P("expert", "tensor", None),
        ),
        check_vma=False,
    )
```

```python
import jax
import jax.numpy as jnp
from jax import lax
from jax.experimental import pallas as pl
from jax.experimental.pallas import tpu as pltpu
from jax.sharding import PartitionSpec as P

CHUNKS = 2


def _a2a_kernel(x_ref, o_ref, send_sem, recv_sem, local_sem):
    n = x_ref.shape[0]
    me = lax.axis_index("expert")
    tau = lax.axis_index("tensor")
    barrier = pltpu.get_barrier_semaphore()

    def greet(k, carry):
        peer = lax.rem(me + k, n)
        pl.semaphore_signal(
            barrier, inc=1, device_id=(peer, tau), device_id_type=pl.DeviceIdType.MESH
        )
        return carry

    lax.fori_loop(1, n, greet, 0)
    pl.semaphore_wait(barrier, n - 1)

    local = pltpu.make_async_copy(x_ref.at[me], o_ref.at[me], local_sem)
    local.start()

    def push(i, carry):
        half = i // 2 + 1
        k = half + (i % 2) * (n - 2 * half)
        peer = lax.rem(me + k, n)
        pltpu.make_async_remote_copy(
            src_ref=x_ref.at[peer],
            dst_ref=o_ref.at[me],
            send_sem=send_sem.at[k],
            recv_sem=recv_sem.at[k],
            device_id=(peer, tau),
            device_id_type=pl.DeviceIdType.MESH,
        ).start()
        return carry

    lax.fori_loop(0, n - 1, push, 0)

    def settle(k, carry):
        peer = lax.rem(me + k, n)
        source = lax.rem(me + n - k, n)
        pltpu.make_async_remote_copy(
            src_ref=x_ref.at[peer],
            dst_ref=o_ref.at[source],
            send_sem=send_sem.at[k],
            recv_sem=recv_sem.at[k],
            device_id=(peer, tau),
            device_id_type=pl.DeviceIdType.MESH,
        ).wait()
        return carry

    lax.fori_loop(1, n, settle, 0)
    local.wait()


def expert_all_to_all(x, collective_id):
    n = x.shape[0]
    return pl.pallas_call(
        _a2a_kernel,
        out_shape=jax.ShapeDtypeStruct(x.shape, x.dtype),
        in_specs=[pl.BlockSpec(memory_space=pl.ANY)],
        out_specs=pl.BlockSpec(memory_space=pl.ANY),
        scratch_shapes=[
            pltpu.SemaphoreType.DMA((n,)),
            pltpu.SemaphoreType.DMA((n,)),
            pltpu.SemaphoreType.DMA(()),
        ],
        compiler_params=pltpu.CompilerParams(collective_id=collective_id, has_side_effects=True),
        cost_estimate=pl.CostEstimate(
            flops=0, transcendentals=0, bytes_accessed=2 * x.size * x.dtype.itemsize
        ),
    )(x)


def expert_chunk(rows, scaled, w_in, w_out, quarter, ids):
    slots = rows.shape[2]
    send = jnp.concatenate([rows, scaled], axis=2)
    arrived = expert_all_to_all(send.reshape(send.shape[0], -1, quarter), ids[0]).reshape(send.shape)
    whole = lax.all_gather(arrived, "tensor", axis=3, tiled=True)
    expert_rows = whole[:, :, :slots]
    expert_scaled = whole[:, :, slots:]
    preact = jnp.einsum("nesd,edh->nesh", expert_rows, w_in, preferred_element_type=jnp.float32)
    sigmoid_val = jax.nn.sigmoid(preact)
    hidden = (preact * sigmoid_val).astype(jnp.bfloat16)
    out_part = jnp.einsum("nesh,ehd->nesd", hidden, w_out, preferred_element_type=jnp.float32)
    grad_hidden = jnp.einsum(
        "nesd,ehd->nesh", expert_scaled, w_out, preferred_element_type=jnp.float32
    )
    grad_preact = (grad_hidden * sigmoid_val * (1.0 + preact * (1.0 - sigmoid_val))).astype(
        jnp.bfloat16
    )
    d_w_out = jnp.einsum(
        "nesh,nesd->ehd", hidden, expert_scaled, preferred_element_type=jnp.float32
    )
    d_w_in = jnp.einsum(
        "nesd,nesh->edh", expert_rows, grad_preact, preferred_element_type=jnp.float32
    )
    grad_part = jnp.einsum("nesh,edh->nesd", grad_preact, w_in, preferred_element_type=jnp.float32)
    parts = jnp.concatenate(
        [out_part.astype(jnp.bfloat16), grad_part.astype(jnp.bfloat16)], axis=2
    )
    sums = lax.psum_scatter(parts, "tensor", scatter_dimension=3, tiled=True)
    back = expert_all_to_all(sums.reshape(sums.shape[0], -1, quarter), ids[1]).reshape(sums.shape)
    return back[:, :, :slots], back[:, :, slots:], d_w_in, d_w_out


def shards(tokens, cotangent, routing, gates, w_in, w_out):
    devices = lax.axis_size("expert")
    local_experts = w_in.shape[0]
    experts = devices * local_experts
    tok_rows = routing.shape[0]
    capacity = tok_rows // 4
    buffer_rows = experts * capacity
    highest = lax.Precision.HIGHEST
    matches = (routing[:, :, None] == jnp.arange(experts, dtype=jnp.int32)[None, None, :]).astype(
        jnp.int32
    )
    per_token = jnp.sum(matches, axis=1)
    earlier = jnp.cumsum(per_token, axis=0) - per_token
    destination = routing * capacity + jnp.take_along_axis(earlier, routing, axis=1)
    placed = (
        destination[:, :, None] == jnp.arange(buffer_rows, dtype=jnp.int32)[None, None, :]
    ).astype(jnp.float32)
    membership = jnp.sum(placed, axis=1)
    weighting = jnp.sum(placed * gates[:, :, None], axis=1)
    quarter = tokens.shape[1]
    both = jnp.einsum(
        "ktr,ktd->krd",
        jnp.stack([membership, weighting]),
        jnp.stack([tokens, cotangent]).astype(jnp.float32),
        precision=highest,
    ).astype(jnp.bfloat16)
    rows, scaled = both[0], both[1]
    rows = rows.reshape(devices, local_experts, capacity, quarter)
    scaled = scaled.reshape(devices, local_experts, capacity, quarter)
    step = capacity // CHUNKS
    back_out, back_grad, d_w_in, d_w_out = [], [], None, None
    for c in range(CHUNKS):
        window = slice(c * step, (c + 1) * step)
        with jax.named_scope(f"slot_chunk{c}"):
            b_out, b_grad, g_in, g_out = expert_chunk(
                rows[:, :, window], scaled[:, :, window], w_in, w_out, quarter, (2 * c, 2 * c + 1)
            )
        back_out.append(b_out)
        back_grad.append(b_grad)
        d_w_in = g_in if d_w_in is None else d_w_in + g_in
        d_w_out = g_out if d_w_out is None else d_w_out + g_out
    back_out = jnp.concatenate(back_out, axis=2).reshape(buffer_rows, quarter).astype(jnp.float32)
    back_grad = jnp.concatenate(back_grad, axis=2).reshape(buffer_rows, quarter).astype(jnp.float32)
    mixed = jnp.einsum("tr,rd->td", weighting, back_out, precision=highest).astype(jnp.bfloat16)
    d_tokens = jnp.einsum("tr,rd->td", membership, back_grad, precision=highest).astype(
        jnp.bfloat16
    )
    return (mixed, d_tokens, d_w_in.astype(jnp.bfloat16), d_w_out.astype(jnp.bfloat16))


def solution(mesh):
    placed = (
        P("expert", "tensor"),
        P("expert", "tensor"),
        P("expert", None),
        P("expert", None),
        P("expert", None, "tensor"),
        P("expert", "tensor", None),
    )
    return jax.shard_map(
        shards,
        mesh=mesh,
        in_specs=placed,
        out_specs=(
            P("expert", "tensor"),
            P("expert", "tensor"),
            P("expert", None, "tensor"),
            P("expert", "tensor", None),
        ),
        check_vma=False,
    )
```
